512 devices in a mesh: tok: 64 (over y, z), head: 8 (over x, core).
Axes of the slice: x: 4, y: 4, z: 16, core: 2. Of those that a mesh axis runs over, the one named last changes fastest.
Arguments:
- source_keys: bfloat16 [16384, 2048], P('tok', 'head'), may hold values from -6 to 6
- source_values: bfloat16 [16384, 2048], P('tok', 'head'), may hold values from -6 to 6
- queries: bfloat16 [16384, 2048], P('tok', 'head'), may hold values from -6 to 6
- fast_weights: float32 [3, 16, 128, 512], P(None, 'head'), may hold values from -0.5 to 0.5
- step_size: float32 [16], P('head'), may hold values from 0.3 to 3
- edit_mask: int32 [64], P('tok'), may hold values 0 or 1
- out_proj: bfloat16 [2048, 2048], P(None, 'head'), may hold values from -0.125 to 0.125
Outputs:
- layer_out: bfloat16 [16384, 2048], P('tok', 'head')
The draws below stay inside these ranges and needn't reach their ends.
Inputs may be any that keep to these rules, and one draw needn't show every extreme that they name: `edit_mask`: 1 marks a block of source frames whose keys and values update the fast weights, 0 a block of edited frames.
All inputs are finite; a program needn't handle non-finite values.
Results may differ from the reference program's by a relative error of at most 0.0087.
Values may be sent and summed in bfloat16 or wider, within the bound.
A program may use at most 64 MiB of HBM per device.

```python
import math
import jax
import jax.numpy as jnp
from jax import lax

D = 2048
H = 16
FF = 512
DH = 128
BLOCK = 256
ITERS = 5
TOKENS = 16384
BLOCKS = 64


def touch_ends(result, key, smallest, top_value):
    longest = result.shape.index(max(result.shape))
    spots = []
    for shift in (0, 1):
        where = [jax.random.randint(jax.random.fold_in(key, axis), (), 0, length) for axis, length in enumerate(result.shape)]
        where[longest] = (where[longest] + shift) % result.shape[longest]
        spots.append(tuple(where))
    return result.at[spots[0]].set(smallest).at[spots[1]].set(top_value)


def steps_of(own_key, shape, cuts, least, largest):
    def one(position, blocks):
        heights = jax.random.uniform(jax.random.fold_in(jax.random.fold_in(own_key, 6), position), (blocks,), jnp.float32, least / len(cuts), largest / len(cuts))
        return jnp.repeat(jnp.exp(heights), shape[position] // blocks).reshape((-1,) + (1,) * (len(shape) - position - 1))

    level = one(*cuts[0])
    for cut in cuts[1:]:
        level = level * one(*cut)
    return level


def scatter_about(rng, shape, width, reach, shards=(), kind=jnp.bfloat16):
    drawn = jax.random.normal(rng, shape, jnp.float32) * width
    if len(shards) > 0:
        drawn = steps_of(rng, shape, shards, -0.22, 0.18) * drawn
    return jnp.clip(drawn, min=-reach, max=reach).astype(kind)


def setup_inputs(seed: int = 0) -> dict:
    key_list = jax.random.split(jax.random.key(seed), 8)
    source_keys = scatter_about(key_list[0], (TOKENS, D), 1.0, 6.0, ((0, 64), (1, 8)))
    source_values = scatter_about(key_list[1], (TOKENS, D), 1.0, 6.0, ((0, 64), (1, 8)))
    queries = scatter_about(key_list[2], (TOKENS, D), 1.0, 6.0, ((0, 64), (1, 8)))
    fast_weights = scatter_about(key_list[3], (3, H, DH, FF), DH ** -0.5, 0.5, ((1, 8),), jnp.float32)
    step_size = jnp.clip(jnp.exp(math.log(3.0) - 2.3025851 * jax.random.uniform(key_list[4], (H,), jnp.float32) ** steps_of(key_list[4], (H,), ((0, 8),), -0.2, 0.2)), 0.3, 3.0)
    edit_mask = touch_ends((jax.random.randint(key_list[5], (BLOCKS,), 0, 2) < 1).astype(jnp.int32), jax.random.fold_in(key_list[5], 1), 0, 1)
    out_proj = scatter_about(key_list[6], (D, D), D ** -0.5, 0.125, ((1, 8),))
    return {"source_keys": source_keys, "source_values": source_values, "queries": queries, "fast_weights": fast_weights, "step_size": step_size, "edit_mask": edit_mask, "out_proj": out_proj}


coef_a = 3.4445
coef_b = -4.775
coef_c = 2.0315
highest = lax.Precision.HIGHEST

def silu_grad(preact):
    sigmoid_value = jax.nn.sigmoid(preact)
    return sigmoid_value * (1.0 + preact * (1.0 - sigmoid_value))

def orthogonalize(gradients):
    scaling = lax.rsqrt(lax.optimization_barrier(jnp.sum(gradients * gradients, axis=(-2, -1), keepdims=True)) + 1e-06)
    iterate = gradients * scaling
    for sweeps in range(ITERS):
        gram_matrix = jnp.einsum('...if,...jf->...ij', iterate, iterate, precision=highest)
        polynomial = coef_b * gram_matrix + coef_c * jnp.einsum('...ij,...jk->...ik', gram_matrix, gram_matrix, precision=highest)
        iterate = coef_a * iterate + jnp.einsum('...ij,...jf->...if', polynomial, iterate, precision=highest)
    return iterate

def renormalize(previous, proposed):
    old_norm = jnp.sqrt(lax.optimization_barrier(jnp.sum(previous * previous, axis=-2, keepdims=True)) + 1e-06)
    new_norm = jnp.sqrt(lax.optimization_barrier(jnp.sum(proposed * proposed, axis=-2, keepdims=True)) + 1e-06)
    return proposed * (old_norm / new_norm)

def head_step(operands):
    keys_head, values_head, query_head, weights, rate_head = operands
    weights_low = weights.astype(jnp.bfloat16)
    gate_pre = jnp.dot(keys_head, weights_low[0], preferred_element_type=jnp.float32)
    up_pre = jnp.dot(keys_head, weights_low[2], preferred_element_type=jnp.float32)
    hidden = (jax.nn.silu(gate_pre) * up_pre).astype(jnp.bfloat16)
    back_grad = jnp.dot(values_head, weights_low[1], preferred_element_type=jnp.float32)
    gate_grad = (back_grad * up_pre * silu_grad(gate_pre)).astype(jnp.bfloat16)
    up_grad = (back_grad * jax.nn.silu(gate_pre)).astype(jnp.bfloat16)
    grad_gate = jnp.dot(keys_head.T, gate_grad, preferred_element_type=jnp.float32)
    grad_down = jnp.dot(values_head.T, hidden, preferred_element_type=jnp.float32)
    grad_up = jnp.dot(keys_head.T, up_grad, preferred_element_type=jnp.float32)
    gradients = jnp.stack([grad_gate, grad_down, grad_up])
    directions = orthogonalize(gradients)
    updated = renormalize(weights, weights + rate_head * directions).astype(jnp.bfloat16)
    read_gate = jnp.dot(query_head, updated[0], preferred_element_type=jnp.float32)
    read_up = jnp.dot(query_head, updated[2], preferred_element_type=jnp.float32)
    read_hidden = (jax.nn.silu(read_gate) * read_up).astype(jnp.bfloat16)
    return jnp.dot(read_hidden, updated[1].T, preferred_element_type=jnp.float32).astype(jnp.bfloat16)

def reference(source_keys, source_values, queries, fast_weights, step_size, edit_mask, out_proj):
    token_mask = jnp.repeat(edit_mask, BLOCK).astype(jnp.bfloat16)
    keys_heads = jnp.moveaxis(source_keys.reshape(TOKENS, H, DH), 1, 0)
    masked_values = source_values.reshape(TOKENS, H, DH) * token_mask[:, None, None]
    values_heads = jnp.moveaxis(masked_values, 1, 0)
    query_heads = jnp.moveaxis(queries.reshape(TOKENS, H, DH), 1, 0)
    weight_heads = jnp.moveaxis(fast_weights, 1, 0)
    reads = lax.map(head_step, (keys_heads, values_heads, query_heads, weight_heads, step_size))
    read_all = jnp.moveaxis(reads, 0, 1).reshape(TOKENS, D)
    projected = jnp.dot(read_all, out_proj, preferred_element_type=jnp.float32)
    return jax.nn.silu(projected).astype(jnp.bfloat16)
```

```python
import jax
import jax.numpy as jnp
from jax import lax
from jax.experimental import pallas as pl
from jax.experimental.pallas import tpu as pltpu
from jax.sharding import PartitionSpec as P

ITERS = 5
NY = 4
NX = 4
WIN = 4

coef_a = 3.4445
coef_b = -4.775
coef_c = 2.0315

MESH = pl.DeviceIdType.MESH
F32 = jnp.float32
BF16 = jnp.bfloat16


def dot(a, b):
    return jnp.dot(a, b, preferred_element_type=F32)


def dot_nt(a, b):
    return lax.dot_general(a, b, (((1,), (1,)), ((), ())), preferred_element_type=F32)


def dot_tn(a, b):
    return lax.dot_general(a, b, (((0,), (0,)), ((), ())), preferred_element_type=F32)


def split(a):
    high = a.astype(BF16)
    return high, (a - high.astype(F32)).astype(BF16)


def newton_step(iterate):
    rows = iterate.shape[0]
    xh, xl = split(iterate)
    both = dot_nt(xh, jnp.concatenate([xh, xl], axis=0))
    cross = both[:, rows:]
    gram = both[:, :rows] + (cross + cross.T)
    ah, al = split(gram)
    both = dot(ah, jnp.concatenate([ah, al], axis=1))
    cross = both[:, rows:]
    square = both[:, :rows] + (cross + cross.T)
    ph, plo = split(coef_b * gram + coef_c * square)
    return coef_a * iterate + dot(
        jnp.concatenate([ph, plo, ph], axis=1), jnp.concatenate([xh, xh, xl], axis=0)
    )


def kernel(
    nz,
    keys, values, queries, weights, step, mask, proj,
    out,
    kbuf, vraw, vbuf, vother, qbuf, w, whalf, pj,
    acc, gb, rz1, rz2, sb, r4, gfull, xs, new, rf, r,
    lsem, p1s, p1r, p2s, p2r, p3s, p3r, p4s, p4r, fs, fr, xsnd, xrcv, cs, cr, e4, e8,
):
    t = lax.axis_index("tok")
    hd = lax.axis_index("head")
    y = t // nz
    z = t - y * nz
    x = hd // 2
    c = hd - 2 * x
    hs = y // 2
    ch = y - 2 * hs
    oh = 1 - hs
    pair = y + 1 - 2 * ch
    outer = NY - 1 - y
    diag = NY - 1 - pair
    i = lax.rem(z, WIN)

    def dev(yy, zz, xx, cc):
        return (yy * nz + zz, xx * 2 + cc)

    def zp(d):
        return lax.rem(z + d + nz, nz)

    def xp(d):
        return lax.rem(x + d + NX, NX)

    partner = dev(y, z, x, 1 - c)

    def send(src, dst, ss, rs, where):
        copy = pltpu.make_async_remote_copy(
            src_ref=src, dst_ref=dst, send_sem=ss, recv_sem=rs, device_id=where, device_id_type=MESH
        )
        copy.start()
        sent.append(copy)

    def arrived(dst, ss, rs):
        pltpu.make_async_remote_copy(
            src_ref=dst, dst_ref=dst, send_sem=ss, recv_sem=rs, device_id=partner, device_id_type=MESH
        ).wait_recv()

    sent = []

    def local(src, dst, k):
        copy = pltpu.make_async_copy(src, dst, lsem.at[k])
        copy.start()
        return copy

    def cols(a):
        return pl.ds(pl.multiple_of(a * 128, 128), 128)

    barrier = pltpu.get_barrier_semaphore()
    near = [dev(yy, z, x, c) for yy in (pair, outer, diag)]
    near += [dev(y, zp(d), x, c) for d in (1, -1, 2, -2)]
    near += [dev(y, z, xp(d), c) for d in (1, -1, 2)] + [partner]
    for peer in near:
        pl.semaphore_signal(barrier, inc=1, device_id=peer, device_id_type=MESH)

    v_in = [local(values.at[:, cols(hs)], vraw.at[0], 0), local(values.at[:, cols(oh)], vraw.at[1], 1)]
    k_in = local(keys.at[:, cols(hs)], kbuf.at[0], 2)
    wh_in = local(weights.at[:, hs, :, pl.ds(pl.multiple_of(ch * 256, 128), 256)], whalf, 3)
    w_in = local(weights.at[:, hs], w, 4)
    q_in = local(queries.at[:, cols(hs)], qbuf.at[0], 5)
    pj_in = local(proj, pj, 6)

    for copy in v_in:
        copy.wait()
    keep = mask[0].astype(F32)
    vbuf[0] = (vraw[0].astype(F32) * keep).astype(BF16)
    vother[...] = (vraw[1].astype(F32) * keep).astype(BF16)

    pl.semaphore_wait(barrier, len(near))
    to_pair, to_outer, to_diag = (dev(yy, z, x, c) for yy in (pair, outer, diag))
    send(keys.at[:, cols(oh)], kbuf.at[3], p1s.at[2], p1r.at[2], to_diag)
    send(vother, vbuf.at[3], p1s.at[5], p1r.at[5], to_diag)
    send(keys.at[:, cols(hs)], kbuf.at[1], p1s.at[0], p1r.at[0], to_pair)
    send(keys.at[:, cols(oh)], kbuf.at[2], p1s.at[1], p1r.at[1], to_outer)
    send(vbuf.at[0], vbuf.at[1], p1s.at[3], p1r.at[3], to_pair)
    send(vother, vbuf.at[2], p1s.at[4], p1r.at[4], to_outer)
    send(queries.at[:, cols(oh)], qbuf.at[1], p1s.at[6], p1r.at[6], to_outer)
    for d in (2, -2):
        pl.semaphore_signal(e4, inc=1, device_id=dev(y, zp(d), x, c), device_id_type=MESH)

    k_in.wait()
    wh_in.wait()
    low = [whalf[m].astype(BF16) for m in range(3)]
    for s in range(4):
        if s:
            arrived(kbuf.at[s], p1s.at[s - 1], p1r.at[s - 1])
            arrived(vbuf.at[s], p1s.at[s + 2], p1r.at[s + 2])
        k = kbuf[s]
        vm = vbuf[s]
        g = dot(k, low[0])
        u = dot(k, low[2])
        b = dot(vm, low[1])
        sig = jax.nn.sigmoid(g)
        silu = g * sig
        hid = (silu * u).astype(BF16)
        dg = (b * u * (sig * (1.0 + g * (1.0 - sig)))).astype(BF16)
        du = (b * silu).astype(BF16)
        terms = (dot_tn(k, dg), dot_tn(vm, hid), dot_tn(k, du))
        for m in range(3):
            acc[m] = terms[m] if s == 0 else acc[m] + terms[m]
        if s == 0:
            pl.semaphore_wait(e4, 2)
            for d in (4, -4):
                pl.semaphore_signal(e8, inc=1, device_id=dev(y, zp(d), x, c), device_id_type=MESH)

    for j in range(WIN):
        for half in range(2):
            for m in range(3):
                at = 32 * j + 16 * half
                gb[j, half, m] = acc[m, at : at + 16, :].astype(BF16)
    ahead, behind, across = (lax.rem(i + d, WIN) for d in (1, 3, 2))
    send(gb.at[across, 0], rz2.at[0], p2s.at[2], p2r.at[2], dev(y, zp(2), x, c))
    send(gb.at[across, 1], rz2.at[1], p2s.at[3], p2r.at[3], dev(y, zp(-2), x, c))
    send(gb.at[ahead], rz1.at[0], p2s.at[0], p2r.at[0], dev(y, zp(1), x, c))
    send(gb.at[behind], rz1.at[1], p2s.at[1], p2r.at[1], dev(y, zp(-1), x, c))
    for k in range(2):
        arrived(rz1.at[k], p2s.at[k], p2r.at[k])
    for k in range(2):
        arrived(rz2.at[k], p2s.at[2 + k], p2r.at[2 + k])
    sums = {}
    for half in range(2):
        for m in range(3):
            rows = pl.ds(pl.multiple_of(i * 32 + 16 * half, 16), 16)
            total = acc[m, rows, :] + rz1[0, half, m].astype(F32)
            total = total + rz1[1, half, m].astype(F32) + rz2[half, m].astype(F32)
            sums[half, m] = total
            sb[half, m] = total.astype(BF16)
    pl.semaphore_wait(e8, 2)
    send(sb, r4.at[2], p3s.at[2], p3r.at[2], dev(y, zp(8), x, c))
    send(sb, r4.at[0], p3s.at[0], p3r.at[0], dev(y, zp(4), x, c))
    send(sb, r4.at[1], p3s.at[1], p3r.at[1], dev(y, zp(-4), x, c))
    for k in range(3):
        arrived(r4.at[k], p3s.at[k], p3r.at[k])
    for half in range(2):
        for m in range(3):
            total = sums[half, m]
            for k in range(3):
                total = total + r4[k, half, m].astype(F32)
            gfull[ch, i, half, m] = total.astype(BF16)
    mine = gfull.at[ch, i]
    for base, yy in ((4, pair), (0, y)):
        send(gfull.at[ch, i, 0], gfull.at[ch, i, 0], p4s.at[base + 2], p4r.at[base + 2], dev(yy, zp(2), x, c))
        send(gfull.at[ch, i, 1], gfull.at[ch, i, 1], p4s.at[base + 3], p4r.at[base + 3], dev(yy, zp(-2), x, c))
        send(mine, mine, p4s.at[base], p4r.at[base], dev(yy, zp(1), x, c))
        send(mine, mine, p4s.at[base + 1], p4r.at[base + 1], dev(yy, zp(-1), x, c))
    send(mine, mine, p4s.at[8], p4r.at[8], dev(pair, z, x, c))

    w_in.wait()
    old = [jnp.sqrt(jnp.sum(w[m] * w[m], axis=0, keepdims=True) + 1e-06) for m in range(3)]

    arrived(gfull.at[1 - ch, i], p4s.at[8], p4r.at[8])
    for base, side in ((0, ch), (4, 1 - ch)):
        arrived(gfull.at[side, behind], p4s.at[base], p4r.at[base])
        arrived(gfull.at[side, ahead], p4s.at[base + 1], p4r.at[base + 1])
        arrived(gfull.at[side, across, 0], p4s.at[base + 2], p4r.at[base + 2])
        arrived(gfull.at[side, across, 1], p4s.at[base + 3], p4r.at[base + 3])

    for m in range(3):
        columns = [
            jnp.concatenate(
                [gfull[side, j, half, m] for j in range(WIN) for half in range(2)], axis=0
            )
            for side in range(2)
        ]
        grad = jnp.concatenate(columns, axis=1).astype(F32)
        xs[m] = grad * lax.rsqrt(jnp.sum(grad * grad, keepdims=True) + 1e-06)

    @pl.loop(0, ITERS)
    def _(_):
        for m in range(3):
            xs[m] = newton_step(xs[m])

    rate = step[hs]
    for m in range(3):
        proposed = w[m] + rate * xs[m]
        norm = jnp.sqrt(jnp.sum(proposed * proposed, axis=0, keepdims=True) + 1e-06)
        new[m] = (proposed * (old[m] / norm)).astype(BF16)

    def read_of(q):
        rg = dot(q, new[0])
        ru = dot(q, new[2])
        rh = (rg * jax.nn.sigmoid(rg) * ru).astype(BF16)
        return dot_nt(rh, new[1]).astype(BF16)

    around = (0, 1, -1, 2)
    own = 2 * hd + hs
    arrived(qbuf.at[1], p1s.at[6], p1r.at[6])
    rf[...] = read_of(qbuf[1])
    for k in (3, 1, 2, 0):
        send(rf, r.at[own], fs.at[k], fr.at[k], dev(outer, z, xp(around[k]), c))
    q_in.wait()
    r[own] = read_of(qbuf[0])
    for k in (3, 1, 2):
        send(r.at[own], r.at[own], xsnd.at[k - 1], xrcv.at[k - 1], dev(y, z, xp(around[k]), c))
    send(r.at[own], r.at[own], cs.at[0], cr.at[0], partner)
    pj_in.wait()

    def term(block):
        return dot(r[block], pj[pl.ds(pl.multiple_of(block * 128, 128), 128), :])

    def block_of(k, cc, head):
        return 2 * (2 * xp(-around[k]) + cc) + head

    total = term(own)
    for k in range(4):
        block = block_of(k, c, oh)
        arrived(r.at[block], fs.at[k], fr.at[k])
        send(r.at[block], r.at[block], cs.at[4 + k], cr.at[4 + k], partner)
        total = total + term(block)
    for k in range(1, 4):
        block = block_of(k, c, hs)
        arrived(r.at[block], xsnd.at[k - 1], xrcv.at[k - 1])
        send(r.at[block], r.at[block], cs.at[k], cr.at[k], partner)
        total = total + term(block)
    for k, head in [(0, hs)] + [(k, oh) for k in range(4)] + [(k, hs) for k in range(1, 4)]:
        slot = k if head is hs else 4 + k
        block = block_of(k, 1 - c, head)
        arrived(r.at[block], cs.at[slot], cr.at[slot])
        total = total + term(block)
    out[...] = (total * jax.nn.sigmoid(total)).astype(BF16)
    for copy in sent:
        copy.wait_send()


def on_device(nz, source_keys, source_values, queries, fast_weights, step_size, edit_mask, out_proj):
    rows, width = source_keys.shape
    dma = pltpu.SemaphoreType.DMA
    hbm = pl.BlockSpec(memory_space=pl.ANY)
    smem = pl.BlockSpec(memory_space=pltpu.SMEM)

    def body(*refs):
        kernel(nz, *refs)

    return pl.pallas_call(
        body,
        out_shape=jax.ShapeDtypeStruct((rows, width), BF16),
        in_specs=[hbm, hbm, hbm, hbm, smem, smem, hbm],
        out_specs=pl.BlockSpec(memory_space=pltpu.VMEM),
        scratch_shapes=[
            pltpu.VMEM((4, 256, 128), BF16),
            pltpu.VMEM((2, 256, 128), BF16),
            pltpu.VMEM((4, 256, 128), BF16),
            pltpu.VMEM((256, 128), BF16),
            pltpu.VMEM((2, 256, 128), BF16),
            pltpu.VMEM((3, 128, 512), F32),
            pltpu.VMEM((3, 128, 256), F32),
            pltpu.VMEM((2048, 256), BF16),
            pltpu.VMEM((3, 128, 256), F32),
            pltpu.VMEM((4, 2, 3, 16, 256), BF16),
            pltpu.VMEM((2, 2, 3, 16, 256), BF16),
            pltpu.VMEM((2, 3, 16, 256), BF16),
            pltpu.VMEM((2, 3, 16, 256), BF16),
            pltpu.VMEM((3, 2, 3, 16, 256), BF16),
            pltpu.VMEM((2, 4, 2, 3, 16, 256), BF16),
            pltpu.VMEM((3, 128, 512), F32),
            pltpu.VMEM((3, 128, 512), BF16),
            pltpu.VMEM((256, 128), BF16),
            pltpu.VMEM((16, 256, 128), BF16),
            dma((7,)), dma((7,)), dma((7,)), dma((4,)), dma((4,)), dma((3,)), dma((3,)),
            dma((9,)), dma((9,)), dma((4,)), dma((4,)), dma((3,)), dma((3,)), dma((8,)), dma((8,)),
            pltpu.SemaphoreType.REGULAR, pltpu.SemaphoreType.REGULAR,
        ],
        compiler_params=pltpu.CompilerParams(collective_id=0, has_side_effects=True),
        name="lact_step",
    )(source_keys, source_values, queries, fast_weights, step_size, edit_mask, out_proj)


def solution(mesh):
    nz = mesh.shape["tok"] // NY
    in_specs = (
        P("tok", "head"),
        P("tok", "head"),
        P("tok", "head"),
        P(None, "head", None, None),
        P("head"),
        P("tok"),
        P(None, "head"),
    )

    def device_step(*args):
        return on_device(nz, *args)

    return jax.shard_map(
        device_step, mesh=mesh, in_specs=in_specs, out_specs=P("tok", "head"), check_vma=False
    )
```

```python
import jax
import jax.numpy as jnp
from jax import lax
from jax.experimental import pallas as pl
from jax.experimental.pallas import tpu as pltpu
from jax.sharding import PartitionSpec as P

ITERS = 5
NY = 4
NX = 4
WIN = 4

coef_a = 3.4445
coef_b = -4.775
coef_c = 2.0315

MESH = pl.DeviceIdType.MESH
F32 = jnp.float32
BF16 = jnp.bfloat16


def dot(a, b):
    return jnp.dot(a, b, preferred_element_type=F32)


def dot_nt(a, b):
    return lax.dot_general(a, b, (((1,), (1,)), ((), ())), preferred_element_type=F32)


def dot_tn(a, b):
    return lax.dot_general(a, b, (((0,), (0,)), ((), ())), preferred_element_type=F32)


def split(a):
    high = a.astype(BF16)
    return high, (a - high.astype(F32)).astype(BF16)


def three(left, right):
    return dot(
        jnp.concatenate([left[0], left[1], left[0]], axis=1),
        jnp.concatenate([right[0], right[0], right[1]], axis=0),
    )


def orthogonalize(grads):
    rows = grads[0].shape[0]
    on_diagonal = lax.broadcasted_iota(jnp.int32, (rows, rows), 0) == lax.broadcasted_iota(
        jnp.int32, (rows, rows), 1
    )
    eye = jnp.where(on_diagonal, coef_a, 0.0)
    raw = [dot_nt(g, g) for g in grads]
    scales = [
        lax.rsqrt(jnp.sum(jnp.where(on_diagonal, gram, 0.0), keepdims=True) + 1e-06) for gram in raw
    ]
    grams = [gram * (scale * scale) for gram, scale in zip(raw, scales)]
    factors = [None for _ in grads]
    for sweep in range(ITERS):
        halves = [split(gram) for gram in grams]
        squares = [three(half, half) for half in halves]
        polys = [
            split(eye + coef_b * gram + coef_c * square) for gram, square in zip(grams, squares)
        ]
        if sweep == ITERS - 1:
            return [
                three(poly, split(moved)) * scale for poly, moved, scale in zip(polys, parts, scales)
            ]
        if sweep == 0:
            products = [three(poly, half) for poly, half in zip(polys, halves)]
            factors = polys
        else:
            both = [
                three(
                    poly,
                    (
                        jnp.concatenate([half[0], factor[0]], axis=1),
                        jnp.concatenate([half[1], factor[1]], axis=1),
                    ),
                )
                for poly, half, factor in zip(polys, halves, factors)
            ]
            products = [pair[:, :rows] for pair in both]
            factors = [split(pair[:, rows:]) for pair in both]
        grams = [three(split(product), poly) for product, poly in zip(products, polys)]
        if sweep == ITERS - 2:
            parts = [
                dot(jnp.concatenate(factor, axis=1), jnp.concatenate([g, g], axis=0))
                for factor, g in zip(factors, grads)
            ]


def kernel(
    nz,
    keys, values, queries, weights, step, mask, proj,
    out,
    kbuf, vraw, vbuf, vother, qbuf, w, whalf, pj,
    acc, gb, rz1, rz2, sb, r4, gfull, new, rf, r,
    lsem, p1s, p1r, p2s, p2r, p3s, p3r, p4s, p4r, fs, fr, xsnd, xrcv, cs, cr, e4, e8,
):
    t = lax.axis_index("tok")
    hd = lax.axis_index("head")
    y = t // nz
    z = t - y * nz
    x = hd // 2
    c = hd - 2 * x
    hs = y // 2
    ch = y - 2 * hs
    oh = 1 - hs
    pair = y + 1 - 2 * ch
    outer = NY - 1 - y
    diag = NY - 1 - pair
    i = lax.rem(z, WIN)

    def dev(yy, zz, xx, cc):
        return (yy * nz + zz, xx * 2 + cc)

    def zp(d):
        return lax.rem(z + d + nz, nz)

    def xp(d):
        return lax.rem(x + d + NX, NX)

    partner = dev(y, z, x, 1 - c)

    def send(src, dst, ss, rs, where):
        copy = pltpu.make_async_remote_copy(
            src_ref=src, dst_ref=dst, send_sem=ss, recv_sem=rs, device_id=where, device_id_type=MESH
        )
        copy.start()
        sent.append(copy)

    def arrived(dst, ss, rs):
        pltpu.make_async_remote_copy(
            src_ref=dst, dst_ref=dst, send_sem=ss, recv_sem=rs, device_id=partner, device_id_type=MESH
        ).wait_recv()

    sent = []

    def local(src, dst, k):
        copy = pltpu.make_async_copy(src, dst, lsem.at[k])
        copy.start()
        return copy

    def cols(a):
        return pl.ds(pl.multiple_of(a * 128, 128), 128)

    barrier = pltpu.get_barrier_semaphore()
    near = [dev(yy, z, x, c) for yy in (pair, outer, diag)]
    near += [dev(y, zp(d), x, c) for d in (1, -1, 2, -2)]
    near += [dev(y, z, xp(d), c) for d in (1, -1, 2)] + [partner]
    for peer in near:
        pl.semaphore_signal(barrier, inc=1, device_id=peer, device_id_type=MESH)

    v_in = [local(values.at[:, cols(hs)], vraw.at[0], 0), local(values.at[:, cols(oh)], vraw.at[1], 1)]
    k_in = local(keys.at[:, cols(hs)], kbuf.at[0], 2)
    wh_in = local(weights.at[:, hs, :, pl.ds(pl.multiple_of(ch * 256, 128), 256)], whalf, 3)
    w_in = local(weights.at[:, hs], w, 4)
    q_in = local(queries.at[:, cols(hs)], qbuf.at[0], 5)
    pj_in = local(proj, pj, 6)

    for copy in v_in:
        copy.wait()
    keep = mask[0].astype(F32)
    vbuf[0] = (vraw[0].astype(F32) * keep).astype(BF16)
    vother[...] = (vraw[1].astype(F32) * keep).astype(BF16)

    pl.semaphore_wait(barrier, len(near))
    to_pair, to_outer, to_diag = (dev(yy, z, x, c) for yy in (pair, outer, diag))
    send(keys.at[:, cols(oh)], kbuf.at[3], p1s.at[2], p1r.at[2], to_diag)
    send(vother, vbuf.at[3], p1s.at[5], p1r.at[5], to_diag)
    send(keys.at[:, cols(hs)], kbuf.at[1], p1s.at[0], p1r.at[0], to_pair)
    send(keys.at[:, cols(oh)], kbuf.at[2], p1s.at[1], p1r.at[1], to_outer)
    send(vbuf.at[0], vbuf.at[1], p1s.at[3], p1r.at[3], to_pair)
    send(vother, vbuf.at[2], p1s.at[4], p1r.at[4], to_outer)
    for d in (2, -2):
        pl.semaphore_signal(e4, inc=1, device_id=dev(y, zp(d), x, c), device_id_type=MESH)

    k_in.wait()
    wh_in.wait()
    low = [whalf[m].astype(BF16) for m in range(3)]
    for s in range(4):
        if s:
            arrived(kbuf.at[s], p1s.at[s - 1], p1r.at[s - 1])
            arrived(vbuf.at[s], p1s.at[s + 2], p1r.at[s + 2])
        k = kbuf[s]
        vm = vbuf[s]
        g = dot(k, low[0])
        u = dot(k, low[2])
        b = dot(vm, low[1])
        sig = jax.nn.sigmoid(g)
        silu = g * sig
        hid = (silu * u).astype(BF16)
        dg = (b * u * (sig * (1.0 + g * (1.0 - sig)))).astype(BF16)
        du = (b * silu).astype(BF16)
        terms = (dot_tn(k, dg), dot_tn(vm, hid), dot_tn(k, du))
        for m in range(3):
            acc[m] = terms[m] if s == 0 else acc[m] + terms[m]
        if s == 0:
            pl.semaphore_wait(e4, 2)
            for d in (4, -4):
                pl.semaphore_signal(e8, inc=1, device_id=dev(y, zp(d), x, c), device_id_type=MESH)

    ahead, behind, across = (lax.rem(i + d, WIN) for d in (1, 3, 2))
    for m in range(3):
        for j in range(WIN):
            for half in range(2):
                at = 32 * j + 16 * half
                gb[m, j, half] = acc[m, at : at + 16, :].astype(BF16)
    for m in range(3):
        send(gb.at[m, across, 0], rz2.at[m, 0], p2s.at[m, 2], p2r.at[m, 2], dev(y, zp(2), x, c))
        send(gb.at[m, across, 1], rz2.at[m, 1], p2s.at[m, 3], p2r.at[m, 3], dev(y, zp(-2), x, c))
        send(gb.at[m, ahead], rz1.at[m, 0], p2s.at[m, 0], p2r.at[m, 0], dev(y, zp(1), x, c))
        send(gb.at[m, behind], rz1.at[m, 1], p2s.at[m, 1], p2r.at[m, 1], dev(y, zp(-1), x, c))
    send(queries.at[:, cols(oh)], qbuf.at[1], p1s.at[6], p1r.at[6], to_outer)
    pl.semaphore_wait(e8, 2)
    sums = {}
    for m in range(3):
        for k in range(2):
            arrived(rz1.at[m, k], p2s.at[m, k], p2r.at[m, k])
        for k in range(2):
            arrived(rz2.at[m, k], p2s.at[m, 2 + k], p2r.at[m, 2 + k])
        for half in range(2):
            rows = pl.ds(pl.multiple_of(i * 32 + 16 * half, 16), 16)
            total = acc[m, rows, :] + rz1[m, 0, half].astype(F32)
            total = total + rz1[m, 1, half].astype(F32) + rz2[m, half].astype(F32)
            sums[half, m] = total
            sb[m, half] = total.astype(BF16)
        send(sb.at[m], r4.at[m, 2], p3s.at[m, 2], p3r.at[m, 2], dev(y, zp(8), x, c))
        send(sb.at[m], r4.at[m, 0], p3s.at[m, 0], p3r.at[m, 0], dev(y, zp(4), x, c))
        send(sb.at[m], r4.at[m, 1], p3s.at[m, 1], p3r.at[m, 1], dev(y, zp(-4), x, c))
    w_in.wait()
    old = [jnp.sqrt(jnp.sum(w[m] * w[m], axis=0, keepdims=True) + 1e-06) for m in range(3)]
    for m in range(3):
        for k in range(3):
            arrived(r4.at[m, k], p3s.at[m, k], p3r.at[m, k])
        for half in range(2):
            total = sums[half, m]
            for k in range(3):
                total = total + r4[m, k, half].astype(F32)
            gfull[m, ch, i, half] = total.astype(BF16)
        mine, first, second = gfull.at[m, ch, i], gfull.at[m, ch, i, 0], gfull.at[m, ch, i, 1]
        for base, yy in ((4, pair), (0, y)):
            ss, rs = p4s.at[m], p4r.at[m]
            send(first, first, ss.at[base + 2], rs.at[base + 2], dev(yy, zp(2), x, c))
            send(second, second, ss.at[base + 3], rs.at[base + 3], dev(yy, zp(-2), x, c))
            send(mine, mine, ss.at[base], rs.at[base], dev(yy, zp(1), x, c))
            send(mine, mine, ss.at[base + 1], rs.at[base + 1], dev(yy, zp(-1), x, c))
        send(mine, mine, ss.at[8], rs.at[8], dev(pair, z, x, c))
    grads = []
    for m in range(3):
        ss, rs = p4s.at[m], p4r.at[m]
        arrived(gfull.at[m, 1 - ch, i], ss.at[8], rs.at[8])
        for base, side in ((0, ch), (4, 1 - ch)):
            arrived(gfull.at[m, side, behind], ss.at[base], rs.at[base])
            arrived(gfull.at[m, side, ahead], ss.at[base + 1], rs.at[base + 1])
            arrived(gfull.at[m, side, across, 0], ss.at[base + 2], rs.at[base + 2])
            arrived(gfull.at[m, side, across, 1], ss.at[base + 3], rs.at[base + 3])
        columns = [
            jnp.concatenate(
                [gfull[m, side, j, half] for j in range(WIN) for half in range(2)], axis=0
            )
            for side in range(2)
        ]
        grads.append(jnp.concatenate(columns, axis=1))
    directions = orthogonalize(grads)

    rate = step[hs]
    for m in range(3):
        proposed = w[m] + rate * directions[m]
        norm = jnp.sqrt(jnp.sum(proposed * proposed, axis=0, keepdims=True) + 1e-06)
        new[m] = (proposed * (old[m] / norm)).astype(BF16)

    def read_of(q):
        rg = dot(q, new[0])
        ru = dot(q, new[2])
        rh = (rg * jax.nn.sigmoid(rg) * ru).astype(BF16)
        return dot_nt(rh, new[1]).astype(BF16)

    around = (0, 1, -1, 2)
    own = 2 * hd + hs
    arrived(qbuf.at[1], p1s.at[6], p1r.at[6])
    rf[...] = read_of(qbuf[1])
    for k in (3, 1, 2, 0):
        send(rf, r.at[own], fs.at[k], fr.at[k], dev(outer, z, xp(around[k]), c))
    q_in.wait()
    r[own] = read_of(qbuf[0])
    for k in (3, 1, 2):
        send(r.at[own], r.at[own], xsnd.at[k - 1], xrcv.at[k - 1], dev(y, z, xp(around[k]), c))
    send(r.at[own], r.at[own], cs.at[0], cr.at[0], partner)
    pj_in.wait()

    def term(block):
        return dot(r[block], pj[pl.ds(pl.multiple_of(block * 128, 128), 128), :])

    def block_of(k, cc, head):
        return 2 * (2 * xp(-around[k]) + cc) + head

    total = term(own)
    for k in range(4):
        block = block_of(k, c, oh)
        arrived(r.at[block], fs.at[k], fr.at[k])
        send(r.at[block], r.at[block], cs.at[4 + k], cr.at[4 + k], partner)
        total = total + term(block)
    for k in range(1, 4):
        block = block_of(k, c, hs)
        arrived(r.at[block], xsnd.at[k - 1], xrcv.at[k - 1])
        send(r.at[block], r.at[block], cs.at[k], cr.at[k], partner)
        total = total + term(block)
    for k, head in [(0, hs)] + [(k, oh) for k in range(4)] + [(k, hs) for k in range(1, 4)]:
        slot = k if head is hs else 4 + k
        block = block_of(k, 1 - c, head)
        arrived(r.at[block], cs.at[slot], cr.at[slot])
        total = total + term(block)
    out[...] = (total * jax.nn.sigmoid(total)).astype(BF16)
    for copy in sent:
        copy.wait_send()


def on_device(nz, source_keys, source_values, queries, fast_weights, step_size, edit_mask, out_proj):
    rows, width = source_keys.shape
    dma = pltpu.SemaphoreType.DMA
    hbm = pl.BlockSpec(memory_space=pl.ANY)
    smem = pl.BlockSpec(memory_space=pltpu.SMEM)

    def body(*refs):
        kernel(nz, *refs)

    return pl.pallas_call(
        body,
        out_shape=jax.ShapeDtypeStruct((rows, width), BF16),
        in_specs=[hbm, hbm, hbm, hbm, smem, smem, hbm],
        out_specs=pl.BlockSpec(memory_space=pltpu.VMEM),
        scratch_shapes=[
            pltpu.VMEM((4, 256, 128), BF16),
            pltpu.VMEM((2, 256, 128), BF16),
            pltpu.VMEM((4, 256, 128), BF16),
            pltpu.VMEM((256, 128), BF16),
            pltpu.VMEM((2, 256, 128), BF16),
            pltpu.VMEM((3, 128, 512), F32),
            pltpu.VMEM((3, 128, 256), F32),
            pltpu.VMEM((2048, 256), BF16),
            pltpu.VMEM((3, 128, 256), F32),
            pltpu.VMEM((3, 4, 2, 16, 256), BF16),
            pltpu.VMEM((3, 2, 2, 16, 256), BF16),
            pltpu.VMEM((3, 2, 16, 256), BF16),
            pltpu.VMEM((3, 2, 16, 256), BF16),
            pltpu.VMEM((3, 3, 2, 16, 256), BF16),
            pltpu.VMEM((3, 2, 4, 2, 16, 256), BF16),
            pltpu.VMEM((3, 128, 512), BF16),
            pltpu.VMEM((256, 128), BF16),
            pltpu.VMEM((16, 256, 128), BF16),
            dma((7,)), dma((7,)), dma((7,)), dma((3, 4)), dma((3, 4)), dma((3, 3)), dma((3, 3)),
            dma((3, 9)), dma((3, 9)), dma((4,)), dma((4,)), dma((3,)), dma((3,)), dma((8,)), dma((8,)),
            pltpu.SemaphoreType.REGULAR, pltpu.SemaphoreType.REGULAR,
        ],
        compiler_params=pltpu.CompilerParams(collective_id=0, has_side_effects=True),
        name="lact_step",
    )(source_keys, source_values, queries, fast_weights, step_size, edit_mask, out_proj)


def solution(mesh):
    nz = mesh.shape["tok"] // NY
    in_specs = (
        P("tok", "head"),
        P("tok", "head"),
        P("tok", "head"),
        P(None, "head", None, None),
        P("head"),
        P("tok"),
        P(None, "head"),
    )

    def device_step(*args):
        return on_device(nz, *args)

    return jax.shard_map(
        device_step, mesh=mesh, in_specs=in_specs, out_specs=P("tok", "head"), check_vma=False
    )
```

```python
import jax
import jax.numpy as jnp
from jax import lax
from jax.experimental import pallas as pl
from jax.experimental.pallas import tpu as pltpu
from jax.sharding import PartitionSpec as P

ITERS = 5
NY = 4
NX = 4
WIN = 4

coef_a = 3.4445
coef_b = -4.775
coef_c = 2.0315

MESH = pl.DeviceIdType.MESH
F32 = jnp.float32
BF16 = jnp.bfloat16


def dot(a, b):
    return jnp.dot(a, b, preferred_element_type=F32)


def dot_nt(a, b):
    return lax.dot_general(a, b, (((1,), (1,)), ((), ())), preferred_element_type=F32)


def dot_tn(a, b):
    return lax.dot_general(a, b, (((0,), (0,)), ((), ())), preferred_element_type=F32)


def split(a):
    high = a.astype(BF16)
    return high, (a - high.astype(F32)).astype(BF16)


def three(left, right):
    return dot(
        jnp.concatenate([left[0], left[1], left[0]], axis=1),
        jnp.concatenate([right[0], right[0], right[1]], axis=0),
    )


def orthogonalize(grads):
    rows = grads[0].shape[0]
    on_diagonal = lax.broadcasted_iota(jnp.int32, (rows, rows), 0) == lax.broadcasted_iota(
        jnp.int32, (rows, rows), 1
    )
    eye = jnp.where(on_diagonal, coef_a, 0.0)
    raw = [dot_nt(g, g) for g in grads]
    scales = [
        lax.rsqrt(jnp.sum(jnp.where(on_diagonal, gram, 0.0), keepdims=True) + 1e-06) for gram in raw
    ]
    grams = [gram * (scale * scale) for gram, scale in zip(raw, scales)]
    factors = [None for _ in grads]
    for sweep in range(ITERS):
        halves = [split(gram) for gram in grams]
        squares = [three(half, half) for half in halves]
        polys = [
            split(eye + coef_b * gram + coef_c * square) for gram, square in zip(grams, squares)
        ]
        if sweep == ITERS - 1:
            return [
                three(poly, split(moved)) * scale for poly, moved, scale in zip(polys, parts, scales)
            ]
        if sweep == 0:
            products = [three(poly, half) for poly, half in zip(polys, halves)]
            factors = polys
        else:
            both = [
                three(
                    poly,
                    (
                        jnp.concatenate([half[0], factor[0]], axis=1),
                        jnp.concatenate([half[1], factor[1]], axis=1),
                    ),
                )
                for poly, half, factor in zip(polys, halves, factors)
            ]
            products = [pair[:, :rows] for pair in both]
            factors = [split(pair[:, rows:]) for pair in both]
        grams = [three(split(product), poly) for product, poly in zip(products, polys)]
        if sweep == ITERS - 2:
            parts = [
                dot(jnp.concatenate(factor, axis=1), jnp.concatenate([g, g], axis=0))
                for factor, g in zip(factors, grads)
            ]


def kernel(
    nz,
    keys, values, queries, weights, step, mask, proj,
    out,
    kbuf, vraw, vbuf, vother, qbuf, w, pj,
    acc, gb, rz1, rz2, sb, r4, gfull, new, rf, r,
    lsem, p1s, p1r, p2s, p2r, p3s, p3r, p4s, p4r, fs, fr, xsnd, xrcv, cs, cr, e4, e8,
):
    t = lax.axis_index("tok")
    hd = lax.axis_index("head")
    y = t // nz
    z = t - y * nz
    x = hd // 2
    c = hd - 2 * x
    hs = y // 2
    ch = y - 2 * hs
    oh = 1 - hs
    pair = y + 1 - 2 * ch
    outer = NY - 1 - y
    i = lax.rem(z, WIN)

    def dev(yy, zz, xx, cc):
        return (yy * nz + zz, xx * 2 + cc)

    def zp(d):
        return lax.rem(z + d + nz, nz)

    def xp(d):
        return lax.rem(x + d + NX, NX)

    partner = dev(y, z, x, 1 - c)

    def send(src, dst, ss, rs, where):
        copy = pltpu.make_async_remote_copy(
            src_ref=src, dst_ref=dst, send_sem=ss, recv_sem=rs, device_id=where, device_id_type=MESH
        )
        copy.start()
        sent.append(copy)

    def arrived(dst, ss, rs):
        pltpu.make_async_remote_copy(
            src_ref=dst, dst_ref=dst, send_sem=ss, recv_sem=rs, device_id=partner, device_id_type=MESH
        ).wait_recv()

    sent = []

    def local(src, dst, k):
        copy = pltpu.make_async_copy(src, dst, lsem.at[k])
        copy.start()
        return copy

    def cols(a):
        return pl.ds(pl.multiple_of(a * 128, 128), 128)

    barrier = pltpu.get_barrier_semaphore()
    shifts = (0, 1, -1, 2, -2)
    to_outer = dev(outer, z, x, c)
    near = [dev(pair, zp(d), x, c) for d in shifts] + [dev(y, zp(d), x, c) for d in shifts if d]
    near += [dev(y, z, xp(d), c) for d in (1, -1, 2)] + [partner, to_outer]
    for peer in near:
        pl.semaphore_signal(barrier, inc=1, device_id=peer, device_id_type=MESH)

    v_out = local(values.at[:, cols(oh)], vraw.at[1], 0)
    v_in = local(values.at[:, cols(hs)], vraw.at[0], 1)
    k_in = local(keys.at[:, cols(hs)], kbuf.at[0], 2)
    w_in = []
    for side in range(2):
        at = pl.ds(256 * side, 256)
        w_in.append(local(weights.at[:, hs, :, at], w.at[side], 3 + side))
    q_in = local(queries.at[:, cols(hs)], qbuf.at[0], 5)
    pj_in = local(proj, pj, 6)
    keep = mask[0].astype(F32)
    v_out.wait()
    vother[...] = (vraw[1].astype(F32) * keep).astype(BF16)
    v_in.wait()
    vbuf[0] = (vraw[0].astype(F32) * keep).astype(BF16)

    pl.semaphore_wait(barrier, len(near))
    send(keys.at[:, cols(oh)], kbuf.at[1], p1s.at[0], p1r.at[0], to_outer)
    send(vother, vbuf.at[1], p1s.at[1], p1r.at[1], to_outer)
    for d in (2, -2):
        pl.semaphore_signal(e4, inc=1, device_id=dev(y, zp(d), x, c), device_id_type=MESH)

    k_in.wait()
    for copy in w_in:
        copy.wait()
    ahead, behind, across = (lax.rem(i + d, WIN) for d in (1, 3, 2))
    halves = (ch, 1 - ch)

    def gradients(block, side):
        low = [w[side, m].astype(BF16) for m in range(3)]
        k = kbuf[block]
        vm = vbuf[block]
        g = dot(k, low[0])
        u = dot(k, low[2])
        b = dot(vm, low[1])
        sig = jax.nn.sigmoid(g)
        silu = g * sig
        hid = (silu * u).astype(BF16)
        dg = (b * u * (sig * (1.0 + g * (1.0 - sig)))).astype(BF16)
        du = (b * silu).astype(BF16)
        return dot_tn(k, dg), dot_tn(vm, hid), dot_tn(k, du)

    for dy in (1, 0):
        terms = gradients(0, halves[dy])
        for m in range(3):
            acc[dy, m] = terms[m]
    pl.semaphore_wait(e4, 2)
    for d in (4, -4):
        pl.semaphore_signal(e8, inc=1, device_id=dev(y, zp(d), x, c), device_id_type=MESH)
    for k in range(2):
        arrived((kbuf, vbuf)[k].at[1], p1s.at[k], p1r.at[k])
    for dy, yy in ((1, pair), (0, y)):
        terms = gradients(1, halves[dy])
        for m in range(3):
            total = acc[dy, m] + terms[m]
            if dy == 0:
                acc[dy, m] = total
            for j in range(WIN):
                for half in range(2):
                    at = 32 * j + 16 * half
                    gb[dy, j, half, m] = total[at : at + 16, :].astype(BF16)
        ss, rs = p2s.at[dy], p2r.at[dy]
        send(gb.at[dy, across, 0], rz2.at[dy, 0], ss.at[3], rs.at[3], dev(yy, zp(2), x, c))
        send(gb.at[dy, across, 1], rz2.at[dy, 1], ss.at[4], rs.at[4], dev(yy, zp(-2), x, c))
        send(gb.at[dy, ahead], rz1.at[dy, 1], ss.at[1], rs.at[1], dev(yy, zp(1), x, c))
        send(gb.at[dy, behind], rz1.at[dy, 2], ss.at[2], rs.at[2], dev(yy, zp(-1), x, c))
        if dy:
            send(gb.at[dy, i], rz1.at[dy, 0], ss.at[0], rs.at[0], dev(yy, z, x, c))
    send(queries.at[:, cols(oh)], qbuf.at[1], p1s.at[2], p1r.at[2], to_outer)
    pl.semaphore_wait(e8, 2)
    for dy in range(2):
        ss, rs = p2s.at[dy], p2r.at[dy]
        for k in range(3):
            if dy or k:
                arrived(rz1.at[dy, k], ss.at[k], rs.at[k])
        for k in range(2):
            arrived(rz2.at[dy, k], ss.at[3 + k], rs.at[3 + k])
    sums = {}
    for half in range(2):
        for m in range(3):
            rows = pl.ds(pl.multiple_of(i * 32 + 16 * half, 16), 16)
            total = acc[0, m, rows, :]
            for dy in range(2):
                for k in range(3):
                    if dy or k:
                        total = total + rz1[dy, k, half, m].astype(F32)
                total = total + rz2[dy, half, m].astype(F32)
            sums[half, m] = total
            sb[half, m] = total.astype(BF16)
    send(sb, r4.at[2], p3s.at[2], p3r.at[2], dev(y, zp(8), x, c))
    send(sb, r4.at[0], p3s.at[0], p3r.at[0], dev(y, zp(4), x, c))
    send(sb, r4.at[1], p3s.at[1], p3r.at[1], dev(y, zp(-4), x, c))

    def norms(a):
        return jnp.sqrt(jnp.sum(a * a, axis=0, keepdims=True) + 1e-06)

    old = [[norms(w[side, m]) for side in range(2)] for m in range(3)]
    for k in range(3):
        arrived(r4.at[k], p3s.at[k], p3r.at[k])
    for half in range(2):
        for m in range(3):
            total = sums[half, m]
            for k in range(3):
                total = total + r4[k, half, m].astype(F32)
            gfull[ch, i, half, m] = total.astype(BF16)
    mine, first, second = gfull.at[ch, i], gfull.at[ch, i, 0], gfull.at[ch, i, 1]
    for base, yy in ((4, pair), (0, y)):
        send(first, first, p4s.at[base + 2], p4r.at[base + 2], dev(yy, zp(2), x, c))
        send(second, second, p4s.at[base + 3], p4r.at[base + 3], dev(yy, zp(-2), x, c))
        send(mine, mine, p4s.at[base], p4r.at[base], dev(yy, zp(1), x, c))
        send(mine, mine, p4s.at[base + 1], p4r.at[base + 1], dev(yy, zp(-1), x, c))
    send(mine, mine, p4s.at[8], p4r.at[8], dev(pair, z, x, c))
    arrived(gfull.at[1 - ch, i], p4s.at[8], p4r.at[8])
    for base, side in ((0, ch), (4, 1 - ch)):
        arrived(gfull.at[side, behind], p4s.at[base], p4r.at[base])
        arrived(gfull.at[side, ahead], p4s.at[base + 1], p4r.at[base + 1])
        arrived(gfull.at[side, across, 0], p4s.at[base + 2], p4r.at[base + 2])
        arrived(gfull.at[side, across, 1], p4s.at[base + 3], p4r.at[base + 3])
    grads = []
    for m in range(3):
        columns = [
            jnp.concatenate(
                [gfull[side, j, half, m] for j in range(WIN) for half in range(2)], axis=0
            )
            for side in range(2)
        ]
        grads.append(jnp.concatenate(columns, axis=1))
    directions = orthogonalize(grads)

    rate = step[hs]
    for m in range(3):
        for side in range(2):
            at = slice(256 * side, 256 * side + 256)
            proposed = w[side, m] + rate * directions[m][:, at]
            new[m, :, at] = (proposed * (old[m][side] / norms(proposed))).astype(BF16)

    def read_of(q):
        rg = dot(q, new[0])
        ru = dot(q, new[2])
        rh = (rg * jax.nn.sigmoid(rg) * ru).astype(BF16)
        return dot_nt(rh, new[1]).astype(BF16)

    around = (0, 1, -1, 2)
    own = 2 * hd + hs
    arrived(qbuf.at[1], p1s.at[2], p1r.at[2])
    rf[...] = read_of(qbuf[1])
    for k in (3, 1, 2, 0):
        send(rf, r.at[own], fs.at[k], fr.at[k], dev(outer, z, xp(around[k]), c))
    q_in.wait()
    r[own] = read_of(qbuf[0])
    for k in (3, 1, 2):
        send(r.at[own], r.at[own], xsnd.at[k - 1], xrcv.at[k - 1], dev(y, z, xp(around[k]), c))
    send(r.at[own], r.at[own], cs.at[0], cr.at[0], partner)
    pj_in.wait()

    def term(block):
        return dot(r[block], pj[pl.ds(pl.multiple_of(block * 128, 128), 128), :])

    def block_of(k, cc, head):
        return 2 * (2 * xp(-around[k]) + cc) + head

    total = term(own)
    for k in range(4):
        block = block_of(k, c, oh)
        arrived(r.at[block], fs.at[k], fr.at[k])
        send(r.at[block], r.at[block], cs.at[4 + k], cr.at[4 + k], partner)
        total = total + term(block)
    for k in range(1, 4):
        block = block_of(k, c, hs)
        arrived(r.at[block], xsnd.at[k - 1], xrcv.at[k - 1])
        send(r.at[block], r.at[block], cs.at[k], cr.at[k], partner)
        total = total + term(block)
    for k, head in [(0, hs)] + [(k, oh) for k in range(4)] + [(k, hs) for k in range(1, 4)]:
        slot = k if head is hs else 4 + k
        block = block_of(k, 1 - c, head)
        arrived(r.at[block], cs.at[slot], cr.at[slot])
        total = total + term(block)
    out[...] = (total * jax.nn.sigmoid(total)).astype(BF16)
    for copy in sent:
        copy.wait_send()


def on_device(nz, source_keys, source_values, queries, fast_weights, step_size, edit_mask, out_proj):
    rows, width = source_keys.shape
    dma = pltpu.SemaphoreType.DMA
    hbm = pl.BlockSpec(memory_space=pl.ANY)
    smem = pl.BlockSpec(memory_space=pltpu.SMEM)

    def body(*refs):
        kernel(nz, *refs)

    return pl.pallas_call(
        body,
        out_shape=jax.ShapeDtypeStruct((rows, width), BF16),
        in_specs=[hbm, hbm, hbm, hbm, smem, smem, hbm],
        out_specs=pl.BlockSpec(memory_space=pltpu.VMEM),
        scratch_shapes=[
            pltpu.VMEM((2, 256, 128), BF16),
            pltpu.VMEM((2, 256, 128), BF16),
            pltpu.VMEM((2, 256, 128), BF16),
            pltpu.VMEM((256, 128), BF16),
            pltpu.VMEM((2, 256, 128), BF16),
            pltpu.VMEM((2, 3, 128, 256), F32),
            pltpu.VMEM((2048, 256), BF16),
            pltpu.VMEM((2, 3, 128, 256), F32),
            pltpu.VMEM((2, 4, 2, 3, 16, 256), BF16),
            pltpu.VMEM((2, 3, 2, 3, 16, 256), BF16),
            pltpu.VMEM((2, 2, 3, 16, 256), BF16),
            pltpu.VMEM((2, 3, 16, 256), BF16),
            pltpu.VMEM((3, 2, 3, 16, 256), BF16),
            pltpu.VMEM((2, 4, 2, 3, 16, 256), BF16),
            pltpu.VMEM((3, 128, 512), BF16),
            pltpu.VMEM((256, 128), BF16),
            pltpu.VMEM((16, 256, 128), BF16),
            dma((7,)), dma((3,)), dma((3,)), dma((2, 5)), dma((2, 5)), dma((3,)), dma((3,)),
            dma((9,)), dma((9,)), dma((4,)), dma((4,)), dma((3,)), dma((3,)), dma((8,)), dma((8,)),
            pltpu.SemaphoreType.REGULAR, pltpu.SemaphoreType.REGULAR,
        ],
        compiler_params=pltpu.CompilerParams(collective_id=0, has_side_effects=True),
        name="lact_step",
    )(source_keys, source_values, queries, fast_weights, step_size, edit_mask, out_proj)


def solution(mesh):
    nz = mesh.shape["tok"] // NY
    in_specs = (
        P("tok", "head"),
        P("tok", "head"),
        P("tok", "head"),
        P(None, "head", None, None),
        P("head"),
        P("tok"),
        P(None, "head"),
    )

    def device_step(*args):
        return on_device(nz, *args)

    return jax.shard_map(
        device_step, mesh=mesh, in_specs=in_specs, out_specs=P("tok", "head"), check_vma=False
    )
```

```python
import jax
import jax.numpy as jnp
from jax import lax
from jax.experimental import pallas as pl
from jax.experimental.pallas import tpu as pltpu
from jax.sharding import PartitionSpec as P

ITERS = 5
NY = 4
NX = 4
WIN = 4

coef_a = 3.4445
coef_b = -4.775
coef_c = 2.0315

MESH = pl.DeviceIdType.MESH
F32 = jnp.float32
BF16 = jnp.bfloat16


def dot(a, b):
    return jnp.dot(a, b, preferred_element_type=F32)


def dot_nt(a, b):
    return lax.dot_general(a, b, (((1,), (1,)), ((), ())), preferred_element_type=F32)


def dot_tn(a, b):
    return lax.dot_general(a, b, (((0,), (0,)), ((), ())), preferred_element_type=F32)


def split(a):
    high = a.astype(BF16)
    return high, (a - high.astype(F32)).astype(BF16)


def three(left, right):
    return dot(
        jnp.concatenate([left[0], left[1], left[0]], axis=1),
        jnp.concatenate([right[0], right[0], right[1]], axis=0),
    )


def orthogonalize(grads):
    rows = grads[0].shape[0]
    on_diagonal = lax.broadcasted_iota(jnp.int32, (rows, rows), 0) == lax.broadcasted_iota(
        jnp.int32, (rows, rows), 1
    )
    eye = jnp.where(on_diagonal, coef_a, 0.0)
    raw = [dot_nt(g, g) for g in grads]
    scales = [
        lax.rsqrt(jnp.sum(jnp.where(on_diagonal, gram, 0.0), keepdims=True) + 1e-06) for gram in raw
    ]
    grams = [gram * (scale * scale) for gram, scale in zip(raw, scales)]
    factors = [None for _ in grads]
    for sweep in range(ITERS):
        halves = [split(gram) for gram in grams]
        squares = [three(half, half) for half in halves]
        polys = [
            split(eye + coef_b * gram + coef_c * square) for gram, square in zip(grams, squares)
        ]
        if sweep == ITERS - 1:
            return [
                three(poly, split(moved)) * scale for poly, moved, scale in zip(polys, parts, scales)
            ]
        if sweep == 0:
            products = [three(poly, half) for poly, half in zip(polys, halves)]
            factors = polys
        else:
            both = [
                three(
                    poly,
                    (
                        jnp.concatenate([half[0], factor[0]], axis=1),
                        jnp.concatenate([half[1], factor[1]], axis=1),
                    ),
                )
                for poly, half, factor in zip(polys, halves, factors)
            ]
            products = [pair[:, :rows] for pair in both]
            factors = [split(pair[:, rows:]) for pair in both]
        grams = [three(split(product), poly) for product, poly in zip(products, polys)]
        if sweep == ITERS - 2:
            parts = [
                dot(jnp.concatenate(factor, axis=1), jnp.concatenate([g, g], axis=0))
                for factor, g in zip(factors, grads)
            ]


def kernel(
    nz,
    keys, values, queries, weights, step, mask, proj,
    out,
    kbuf, vraw, vbuf, vother, qbuf, w, pj,
    flag, acc, gb, rz1, rz2, sb, r4, gfull, new, rf, r,
    lsem, p1s, p1r, p2s, p2r, p3s, p3r, p4s, p4r, fs, fr, xsnd, xrcv, cs, cr, e2, e4, e8,
):
    t = lax.axis_index("tok")
    hd = lax.axis_index("head")
    y = t // nz
    z = t - y * nz
    x = hd // 2
    c = hd - 2 * x
    hs = y // 2
    ch = y - 2 * hs
    oh = 1 - hs
    pair = y + 1 - 2 * ch
    outer = NY - 1 - y
    i = lax.rem(z, WIN)

    def dev(yy, zz, xx, cc):
        return (yy * nz + zz, xx * 2 + cc)

    def zp(d):
        return lax.rem(z + d + nz, nz)

    def xp(d):
        return lax.rem(x + d + NX, NX)

    partner = dev(y, z, x, 1 - c)

    def send(src, dst, ss, rs, where):
        copy = pltpu.make_async_remote_copy(
            src_ref=src, dst_ref=dst, send_sem=ss, recv_sem=rs, device_id=where, device_id_type=MESH
        )
        copy.start()
        sent.append(copy)

    def arrived(dst, ss, rs):
        pltpu.make_async_remote_copy(
            src_ref=dst, dst_ref=dst, send_sem=ss, recv_sem=rs, device_id=partner, device_id_type=MESH
        ).wait_recv()

    sent = []

    def local(src, dst, k):
        copy = pltpu.make_async_copy(src, dst, lsem.at[k])
        copy.start()
        return copy

    def cols(a):
        return pl.ds(pl.multiple_of(a * 128, 128), 128)

    barrier = pltpu.get_barrier_semaphore()
    to_outer = dev(outer, z, x, c)
    to_pair = dev(pair, z, x, c)
    beside = [dev(y, zp(d), x, c) for d in (1, -1)] + [dev(y, z, xp(d), c) for d in (1, -1)]
    near = beside + [to_outer, to_pair, partner]
    for peer in near:
        pl.semaphore_signal(barrier, inc=1, device_id=peer, device_id_type=MESH)

    mask_in = local(mask, flag, 7)
    v_out = local(values.at[:, cols(oh)], vraw.at[1], 0)
    v_in = local(values.at[:, cols(hs)], vraw.at[0], 1)
    k_in = local(keys.at[:, cols(hs)], kbuf.at[0], 2)
    w_in = []
    for side in range(2):
        at = pl.ds(256 * side, 256)
        w_in.append(local(weights.at[:, hs, :, at], w.at[side], 3 + side))
    q_in = local(queries.at[:, cols(hs)], qbuf.at[0], 5)
    pj_in = local(proj, pj, 6)
    mask_in.wait()
    keep = flag[0].astype(F32)
    v_out.wait()
    vother[...] = (vraw[1].astype(F32) * keep).astype(BF16)
    v_in.wait()
    vbuf[0] = (vraw[0].astype(F32) * keep).astype(BF16)

    pl.semaphore_wait(barrier, len(near))
    send(keys.at[:, cols(oh)], kbuf.at[1], p1s.at[0], p1r.at[0], to_outer)
    send(vother, vbuf.at[1], p1s.at[1], p1r.at[1], to_outer)
    def tell(sem, peers):
        for peer in peers:
            pl.semaphore_signal(sem, inc=1, device_id=peer, device_id_type=MESH)

    tell(e2, beside)

    k_in.wait()
    for copy in w_in:
        copy.wait()
    ahead, behind, across = (lax.rem(i + d, WIN) for d in (1, 3, 2))
    halves = (ch, 1 - ch)

    def gradients(block, side):
        low = [w[side, m].astype(BF16) for m in range(3)]
        k = kbuf[block]
        vm = vbuf[block]
        g = dot(k, low[0])
        u = dot(k, low[2])
        b = dot(vm, low[1])
        sig = jax.nn.sigmoid(g)
        silu = g * sig
        hid = (silu * u).astype(BF16)
        dg = (b * u * (sig * (1.0 + g * (1.0 - sig)))).astype(BF16)
        du = (b * silu).astype(BF16)
        return dot_tn(k, dg), dot_tn(vm, hid), dot_tn(k, du)

    for dy in (1, 0):
        terms = gradients(0, halves[dy])
        for m in range(3):
            acc[dy, m] = terms[m]
        if dy:
            pl.semaphore_wait(e2, len(beside))
            tell(e4, [dev(y, zp(d), x, c) for d in (2, -2)] + [to_pair, to_outer])
    pl.semaphore_wait(e4, 4)
    tell(e8, [dev(y, zp(d), x, c) for d in (4, -4)])
    for k in range(2):
        arrived((kbuf, vbuf)[k].at[1], p1s.at[k], p1r.at[k])
    for dy, yy in ((1, pair), (0, y)):
        terms = gradients(1, halves[dy])
        for m in range(3):
            total = acc[dy, m] + terms[m]
            if dy == 0:
                acc[dy, m] = total
            for j in range(WIN):
                for half in range(2):
                    at = 32 * j + 16 * half
                    gb[dy, j, half, m] = total[at : at + 16, :].astype(BF16)
        ss, rs = p2s.at[dy], p2r.at[dy]
        send(gb.at[dy, across, 0], rz2.at[dy, 0], ss.at[3], rs.at[3], dev(yy, zp(2), x, c))
        send(gb.at[dy, across, 1], rz2.at[dy, 1], ss.at[4], rs.at[4], dev(yy, zp(-2), x, c))
        send(gb.at[dy, ahead], rz1.at[dy, 1], ss.at[1], rs.at[1], dev(yy, zp(1), x, c))
        send(gb.at[dy, behind], rz1.at[dy, 2], ss.at[2], rs.at[2], dev(yy, zp(-1), x, c))
        if dy:
            send(gb.at[dy, i], rz1.at[dy, 0], ss.at[0], rs.at[0], dev(yy, z, x, c))
    send(queries.at[:, cols(oh)], qbuf.at[1], p1s.at[2], p1r.at[2], to_outer)
    pl.semaphore_wait(e8, 2)
    for dy in range(2):
        ss, rs = p2s.at[dy], p2r.at[dy]
        for k in range(3):
            if dy or k:
                arrived(rz1.at[dy, k], ss.at[k], rs.at[k])
        for k in range(2):
            arrived(rz2.at[dy, k], ss.at[3 + k], rs.at[3 + k])
    sums = {}
    for half in range(2):
        for m in range(3):
            rows = pl.ds(pl.multiple_of(i * 32 + 16 * half, 16), 16)
            total = acc[0, m, rows, :]
            for dy in range(2):
                for k in range(3):
                    if dy or k:
                        total = total + rz1[dy, k, half, m].astype(F32)
                total = total + rz2[dy, half, m].astype(F32)
            sums[half, m] = total
            sb[half, m] = total.astype(BF16)
    send(sb, r4.at[2], p3s.at[2], p3r.at[2], dev(y, zp(8), x, c))
    send(sb, r4.at[0], p3s.at[0], p3r.at[0], dev(y, zp(4), x, c))
    send(sb, r4.at[1], p3s.at[1], p3r.at[1], dev(y, zp(-4), x, c))

    def norms(a):
        return jnp.sqrt(jnp.sum(a * a, axis=0, keepdims=True) + 1e-06)

    old = [[norms(w[side, m]) for side in range(2)] for m in range(3)]
    for k in range(3):
        arrived(r4.at[k], p3s.at[k], p3r.at[k])
    for half in range(2):
        for m in range(3):
            total = sums[half, m]
            for k in range(3):
                total = total + r4[k, half, m].astype(F32)
            gfull[ch, i, half, m] = total.astype(BF16)
    mine, first, second = gfull.at[ch, i], gfull.at[ch, i, 0], gfull.at[ch, i, 1]
    for base, yy in ((4, pair), (0, y)):
        send(first, first, p4s.at[base + 2], p4r.at[base + 2], dev(yy, zp(2), x, c))
        send(second, second, p4s.at[base + 3], p4r.at[base + 3], dev(yy, zp(-2), x, c))
        send(mine, mine, p4s.at[base], p4r.at[base], dev(yy, zp(1), x, c))
        send(mine, mine, p4s.at[base + 1], p4r.at[base + 1], dev(yy, zp(-1), x, c))
    send(mine, mine, p4s.at[8], p4r.at[8], dev(pair, z, x, c))
    arrived(gfull.at[1 - ch, i], p4s.at[8], p4r.at[8])
    for base, side in ((0, ch), (4, 1 - ch)):
        arrived(gfull.at[side, behind], p4s.at[base], p4r.at[base])
        arrived(gfull.at[side, ahead], p4s.at[base + 1], p4r.at[base + 1])
        arrived(gfull.at[side, across, 0], p4s.at[base + 2], p4r.at[base + 2])
        arrived(gfull.at[side, across, 1], p4s.at[base + 3], p4r.at[base + 3])
    grads = []
    for m in range(3):
        columns = [
            jnp.concatenate(
                [gfull[side, j, half, m] for j in range(WIN) for half in range(2)], axis=0
            )
            for side in range(2)
        ]
        grads.append(jnp.concatenate(columns, axis=1))
    directions = orthogonalize(grads)

    rate = step[hs]
    for m in range(3):
        for side in range(2):
            at = slice(256 * side, 256 * side + 256)
            proposed = w[side, m] + rate * directions[m][:, at]
            new[m, :, at] = (proposed * (old[m][side] / norms(proposed))).astype(BF16)

    def read_of(q):
        rg = dot(q, new[0])
        ru = dot(q, new[2])
        rh = (rg * jax.nn.sigmoid(rg) * ru).astype(BF16)
        return dot_nt(rh, new[1]).astype(BF16)

    around = (0, 1, -1, 2)
    own = 2 * hd + hs
    arrived(qbuf.at[1], p1s.at[2], p1r.at[2])
    rf[...] = read_of(qbuf[1])
    for k in (3, 1, 2, 0):
        send(rf, r.at[own], fs.at[k], fr.at[k], dev(outer, z, xp(around[k]), c))
    q_in.wait()
    r[own] = read_of(qbuf[0])
    for k in (3, 1, 2):
        send(r.at[own], r.at[own], xsnd.at[k - 1], xrcv.at[k - 1], dev(y, z, xp(around[k]), c))
    send(r.at[own], r.at[own], cs.at[0], cr.at[0], partner)
    pj_in.wait()

    def term(block):
        return dot(r[block], pj[pl.ds(pl.multiple_of(block * 128, 128), 128), :])

    def block_of(k, cc, head):
        return 2 * (2 * xp(-around[k]) + cc) + head

    coming = [(0, 0), (1, 1), (1, 2), (0, 1), (0, 2), (1, 3), (0, 3)]
    for line, k in coming:
        block = block_of(k, c, (oh, hs)[line])
        if line:
            arrived(r.at[block], xsnd.at[k - 1], xrcv.at[k - 1])
        else:
            arrived(r.at[block], fs.at[k], fr.at[k])
        slot = k if line else 4 + k
        send(r.at[block], r.at[block], cs.at[slot], cr.at[slot], partner)
    total = term(own)
    for line, k in coming:
        total = total + term(block_of(k, c, (oh, hs)[line]))
    for line, k in [(1, 0)] + coming:
        slot = k if line else 4 + k
        block = block_of(k, 1 - c, (oh, hs)[line])
        arrived(r.at[block], cs.at[slot], cr.at[slot])
        total = total + term(block)
    out[...] = (total * jax.nn.sigmoid(total)).astype(BF16)
    for copy in sent:
        copy.wait_send()


def on_device(nz, source_keys, source_values, queries, fast_weights, step_size, edit_mask, out_proj):
    rows, width = source_keys.shape
    dma = pltpu.SemaphoreType.DMA
    hbm = pl.BlockSpec(memory_space=pl.ANY)
    smem = pl.BlockSpec(memory_space=pltpu.SMEM)

    def body(*refs):
        kernel(nz, *refs)

    return pl.pallas_call(
        body,
        out_shape=pltpu.VMEM((rows, width), BF16),
        in_specs=[hbm, hbm, hbm, hbm, smem, pl.BlockSpec(memory_space=pltpu.HBM), hbm],
        out_specs=pl.BlockSpec(memory_space=pltpu.VMEM),
        scratch_shapes=[
            pltpu.VMEM((2, 256, 128), BF16),
            pltpu.VMEM((2, 256, 128), BF16),
            pltpu.VMEM((2, 256, 128), BF16),
            pltpu.VMEM((256, 128), BF16),
            pltpu.VMEM((2, 256, 128), BF16),
            pltpu.VMEM((2, 3, 128, 256), F32),
            pltpu.VMEM((2048, 256), BF16),
            pltpu.SMEM((1,), jnp.int32),
            pltpu.VMEM((2, 3, 128, 256), F32),
            pltpu.VMEM((2, 4, 2, 3, 16, 256), BF16),
            pltpu.VMEM((2, 3, 2, 3, 16, 256), BF16),
            pltpu.VMEM((2, 2, 3, 16, 256), BF16),
            pltpu.VMEM((2, 3, 16, 256), BF16),
            pltpu.VMEM((3, 2, 3, 16, 256), BF16),
            pltpu.VMEM((2, 4, 2, 3, 16, 256), BF16),
            pltpu.VMEM((3, 128, 512), BF16),
            pltpu.VMEM((256, 128), BF16),
            pltpu.VMEM((16, 256, 128), BF16),
            dma((8,)), dma((3,)), dma((3,)), dma((2, 5)), dma((2, 5)), dma((3,)), dma((3,)),
            dma((9,)), dma((9,)), dma((4,)), dma((4,)), dma((3,)), dma((3,)), dma((8,)), dma((8,)),
            pltpu.SemaphoreType.REGULAR, pltpu.SemaphoreType.REGULAR, pltpu.SemaphoreType.REGULAR,
        ],
        compiler_params=pltpu.CompilerParams(collective_id=0, has_side_effects=True),
        name="lact_step",
    )(source_keys, source_values, queries, fast_weights, step_size, edit_mask, out_proj)


def solution(mesh):
    nz = mesh.shape["tok"] // NY
    in_specs = (
        P("tok", "head"),
        P("tok", "head"),
        P("tok", "head"),
        P(None, "head", None, None),
        P("head"),
        P("tok"),
        P(None, "head"),
    )

    def device_step(*args):
        return on_device(nz, *args)

    return jax.shard_map(
        device_step, mesh=mesh, in_specs=in_specs, out_specs=P("tok", "head"), check_vma=False
    )
```

```python
import jax
import jax.numpy as jnp
from jax import lax
from jax.experimental import pallas as pl
from jax.experimental.pallas import tpu as pltpu
from jax.sharding import PartitionSpec as P

ITERS = 5
NY = 4
NX = 4
WIN = 4

coef_a = 3.4445
coef_b = -4.775
coef_c = 2.0315

MESH = pl.DeviceIdType.MESH
F32 = jnp.float32
BF16 = jnp.bfloat16


def dot(a, b):
    return jnp.dot(a, b, preferred_element_type=F32)


def dot_nt(a, b):
    return lax.dot_general(a, b, (((1,), (1,)), ((), ())), preferred_element_type=F32)


def dot_tn(a, b):
    return lax.dot_general(a, b, (((0,), (0,)), ((), ())), preferred_element_type=F32)


def split(a):
    high = a.astype(BF16)
    return high, (a - high.astype(F32)).astype(BF16)


def three(left, right):
    return dot(
        jnp.concatenate([left[0], left[1], left[0]], axis=1),
        jnp.concatenate([right[0], right[0], right[1]], axis=0),
    )


def orthogonalize(grads):
    rows = grads[0].shape[0]
    on_diagonal = lax.broadcasted_iota(jnp.int32, (rows, rows), 0) == lax.broadcasted_iota(
        jnp.int32, (rows, rows), 1
    )
    eye = jnp.where(on_diagonal, coef_a, 0.0)
    raw = [dot_nt(g, g) for g in grads]
    scales = [
        lax.rsqrt(jnp.sum(jnp.where(on_diagonal, gram, 0.0), keepdims=True) + 1e-06) for gram in raw
    ]
    grams = [gram * (scale * scale) for gram, scale in zip(raw, scales)]
    factors = [None for _ in grads]
    for sweep in range(ITERS):
        halves = [split(gram) for gram in grams]
        squares = [three(half, half) for half in halves]
        polys = [
            split(eye + coef_b * gram + coef_c * square) for gram, square in zip(grams, squares)
        ]
        if sweep == ITERS - 1:
            return [
                three(poly, split(moved)) * scale for poly, moved, scale in zip(polys, parts, scales)
            ]
        if sweep == 0:
            products = [three(poly, half) for poly, half in zip(polys, halves)]
            factors = polys
        else:
            both = [
                three(
                    poly,
                    (
                        jnp.concatenate([half[0], factor[0]], axis=1),
                        jnp.concatenate([half[1], factor[1]], axis=1),
                    ),
                )
                for poly, half, factor in zip(polys, halves, factors)
            ]
            products = [pair[:, :rows] for pair in both]
            factors = [split(pair[:, rows:]) for pair in both]
        grams = [three(split(product), poly) for product, poly in zip(products, polys)]
        if sweep == ITERS - 2:
            parts = [
                dot(jnp.concatenate(factor, axis=1), jnp.concatenate([g, g], axis=0))
                for factor, g in zip(factors, grads)
            ]


def kernel(
    nz,
    keys, values, queries, weights, step, mask, proj,
    out,
    kbuf, vraw, vbuf, vother, qbuf, w, pj,
    flag, acc, gb, rz1, rz2, sb, r4, gfull, new, rf, r,
    lsem, p1s, p1r, p2s, p2r, p3s, p3r, p4s, p4r, fs, fr, xsnd, xrcv, cs, cr, e2, e4, e8,
):
    t = lax.axis_index("tok")
    hd = lax.axis_index("head")
    y = t // nz
    z = t - y * nz
    x = hd // 2
    c = hd - 2 * x
    hs = y // 2
    ch = y - 2 * hs
    oh = 1 - hs
    pair = y + 1 - 2 * ch
    outer = NY - 1 - y
    i = lax.rem(z, WIN)

    def dev(yy, zz, xx, cc):
        return (yy * nz + zz, xx * 2 + cc)

    def zp(d):
        return lax.rem(z + d + nz, nz)

    def xp(d):
        return lax.rem(x + d + NX, NX)

    partner = dev(y, z, x, 1 - c)

    def send(src, dst, ss, rs, where):
        copy = pltpu.make_async_remote_copy(
            src_ref=src, dst_ref=dst, send_sem=ss, recv_sem=rs, device_id=where, device_id_type=MESH
        )
        copy.start()
        sent.append(copy)

    def arrived(dst, ss, rs):
        pltpu.make_async_remote_copy(
            src_ref=dst, dst_ref=dst, send_sem=ss, recv_sem=rs, device_id=partner, device_id_type=MESH
        ).wait_recv()

    sent = []

    def local(src, dst, k):
        copy = pltpu.make_async_copy(src, dst, lsem.at[k])
        copy.start()
        return copy

    def cols(a):
        return pl.ds(pl.multiple_of(a * 128, 128), 128)

    barrier = pltpu.get_barrier_semaphore()
    to_outer = dev(outer, z, x, c)
    to_pair = dev(pair, z, x, c)
    beside = [dev(y, zp(d), x, c) for d in (1, -1)] + [dev(y, z, xp(d), c) for d in (1, -1)]
    near = beside + [to_outer, to_pair, partner]
    for peer in near:
        pl.semaphore_signal(barrier, inc=1, device_id=peer, device_id_type=MESH)

    mask_in = local(mask, flag, 7)
    v_out = local(values.at[:, cols(oh)], vraw.at[1], 0)
    v_in = local(values.at[:, cols(hs)], vraw.at[0], 1)
    k_in = local(keys.at[:, cols(hs)], kbuf.at[0], 2)
    w_in = []
    for side in range(2):
        at = pl.ds(256 * side, 256)
        w_in.append(local(weights.at[:, hs, :, at], w.at[side], 3 + side))
    q_in = local(queries.at[:, cols(hs)], qbuf.at[0], 5)
    pj_in = local(proj, pj, 6)
    mask_in.wait()
    keep = flag[0].astype(F32)
    v_out.wait()
    vother[...] = (vraw[1].astype(F32) * keep).astype(BF16)
    v_in.wait()
    vbuf[0] = (vraw[0].astype(F32) * keep).astype(BF16)

    pl.semaphore_wait(barrier, len(near))
    send(keys.at[:, cols(oh)], kbuf.at[1], p1s.at[0], p1r.at[0], to_outer)
    send(vother, vbuf.at[1], p1s.at[1], p1r.at[1], to_outer)
    def tell(sem, peers):
        for peer in peers:
            pl.semaphore_signal(sem, inc=1, device_id=peer, device_id_type=MESH)

    tell(e2, beside)

    k_in.wait()
    for copy in w_in:
        copy.wait()
    ahead, behind, across = (lax.rem(i + d, WIN) for d in (1, 3, 2))
    halves = (ch, 1 - ch)

    def gradients(block, side):
        low = [w[side, m].astype(BF16) for m in range(3)]
        k = kbuf[block]
        vm = vbuf[block]
        g = dot(k, low[0])
        u = dot(k, low[2])
        b = dot(vm, low[1])
        sig = jax.nn.sigmoid(g)
        silu = g * sig
        hid = (silu * u).astype(BF16)
        dg = (b * u * (sig * (1.0 + g * (1.0 - sig)))).astype(BF16)
        du = (b * silu).astype(BF16)
        return dot_tn(k, dg), dot_tn(vm, hid), dot_tn(k, du)

    for dy in (1, 0):
        terms = gradients(0, halves[dy])
        for m in range(3):
            acc[dy, m] = terms[m]
        if dy:
            pl.semaphore_wait(e2, len(beside))
            tell(e4, [dev(y, zp(d), x, c) for d in (2, -2)] + [to_pair, to_outer])
    pl.semaphore_wait(e4, 4)
    tell(e8, [dev(y, zp(d), x, c) for d in (4, -4)])
    for k in range(2):
        arrived((kbuf, vbuf)[k].at[1], p1s.at[k], p1r.at[k])
    for dy, yy in ((1, pair), (0, y)):
        terms = gradients(1, halves[dy])
        for m in range(3):
            total = acc[dy, m] + terms[m]
            if dy == 0:
                acc[dy, m] = total
            for j in range(WIN):
                for half in range(2):
                    at = 32 * j + 16 * half
                    gb[dy, j, half, m] = total[at : at + 16, :].astype(BF16)
        ss, rs = p2s.at[dy], p2r.at[dy]
        send(gb.at[dy, across, 0], rz2.at[dy, 0], ss.at[3], rs.at[3], dev(yy, zp(2), x, c))
        send(gb.at[dy, across, 1], rz2.at[dy, 1], ss.at[4], rs.at[4], dev(yy, zp(-2), x, c))
        send(gb.at[dy, ahead], rz1.at[dy, 1], ss.at[1], rs.at[1], dev(yy, zp(1), x, c))
        send(gb.at[dy, behind], rz1.at[dy, 2], ss.at[2], rs.at[2], dev(yy, zp(-1), x, c))
        if dy:
            send(gb.at[dy, i], rz1.at[dy, 0], ss.at[0], rs.at[0], dev(yy, z, x, c))
    send(queries.at[:, cols(oh)], qbuf.at[1], p1s.at[2], p1r.at[2], to_outer)
    pl.semaphore_wait(e8, 2)
    for dy in range(2):
        ss, rs = p2s.at[dy], p2r.at[dy]
        for k in range(3):
            if dy or k:
                arrived(rz1.at[dy, k], ss.at[k], rs.at[k])
        for k in range(2):
            arrived(rz2.at[dy, k], ss.at[3 + k], rs.at[3 + k])
    sums = {}
    for half in range(2):
        for m in range(3):
            rows = pl.ds(pl.multiple_of(i * 32 + 16 * half, 16), 16)
            total = acc[0, m, rows, :]
            for dy in range(2):
                for k in range(3):
                    if dy or k:
                        total = total + rz1[dy, k, half, m].astype(F32)
                total = total + rz2[dy, half, m].astype(F32)
            sums[half, m] = total
            sb[half, m] = total.astype(BF16)
    send(sb, r4.at[2], p3s.at[2], p3r.at[2], dev(y, zp(8), x, c))
    sent.pop().wait_send()
    send(sb, r4.at[0], p3s.at[0], p3r.at[0], dev(y, zp(4), x, c))
    send(sb, r4.at[1], p3s.at[1], p3r.at[1], dev(y, zp(-4), x, c))

    def norms(a):
        return jnp.sqrt(jnp.sum(a * a, axis=0, keepdims=True) + 1e-06)

    old = [[norms(w[side, m]) for side in range(2)] for m in range(3)]
    for k in range(3):
        arrived(r4.at[k], p3s.at[k], p3r.at[k])
    for half in range(2):
        for m in range(3):
            total = sums[half, m]
            for k in range(3):
                total = total + r4[k, half, m].astype(F32)
            gfull[ch, i, half, m] = total.astype(BF16)
    mine, first, second = gfull.at[ch, i], gfull.at[ch, i, 0], gfull.at[ch, i, 1]
    for base, yy in ((4, pair), (0, y)):
        send(first, first, p4s.at[base + 2], p4r.at[base + 2], dev(yy, zp(2), x, c))
        send(second, second, p4s.at[base + 3], p4r.at[base + 3], dev(yy, zp(-2), x, c))
        send(mine, mine, p4s.at[base], p4r.at[base], dev(yy, zp(1), x, c))
        send(mine, mine, p4s.at[base + 1], p4r.at[base + 1], dev(yy, zp(-1), x, c))
    send(mine, mine, p4s.at[8], p4r.at[8], dev(pair, z, x, c))
    arrived(gfull.at[1 - ch, i], p4s.at[8], p4r.at[8])
    for base, side in ((0, ch), (4, 1 - ch)):
        arrived(gfull.at[side, behind], p4s.at[base], p4r.at[base])
        arrived(gfull.at[side, ahead], p4s.at[base + 1], p4r.at[base + 1])
        arrived(gfull.at[side, across, 0], p4s.at[base + 2], p4r.at[base + 2])
        arrived(gfull.at[side, across, 1], p4s.at[base + 3], p4r.at[base + 3])
    grads = []
    for m in range(3):
        columns = [
            jnp.concatenate(
                [gfull[side, j, half, m] for j in range(WIN) for half in range(2)], axis=0
            )
            for side in range(2)
        ]
        grads.append(jnp.concatenate(columns, axis=1))
    directions = orthogonalize(grads)

    rate = step[hs]
    for m in range(3):
        for side in range(2):
            at = slice(256 * side, 256 * side + 256)
            proposed = w[side, m] + rate * directions[m][:, at]
            new[m, :, at] = (proposed * (old[m][side] / norms(proposed))).astype(BF16)

    def read_of(q):
        rg = dot(q, new[0])
        ru = dot(q, new[2])
        rh = (rg * jax.nn.sigmoid(rg) * ru).astype(BF16)
        return dot_nt(rh, new[1]).astype(BF16)

    around = (0, 1, -1, 2)
    own = 2 * hd + hs
    arrived(qbuf.at[1], p1s.at[2], p1r.at[2])
    for half in range(2):
        part = pl.ds(128 * half, 128)
        rf[part, :] = read_of(qbuf[1, part, :])
        for k in (3, 1, 2, 0):
            where = dev(outer, z, xp(around[k]), c)
            send(rf.at[part], r.at[own, part], fs.at[k, half], fr.at[k, half], where)
    q_in.wait()
    r[own] = read_of(qbuf[0])
    for k in (3, 1, 2):
        send(r.at[own], r.at[own], xsnd.at[k - 1], xrcv.at[k - 1], dev(y, z, xp(around[k]), c))
    send(r.at[own], r.at[own], cs.at[0], cr.at[0], partner)
    pj_in.wait()

    def term(block):
        return dot(r[block], pj[pl.ds(pl.multiple_of(block * 128, 128), 128), :])

    def block_of(k, cc, head):
        return 2 * (2 * xp(-around[k]) + cc) + head

    coming = [(0, 0), (1, 1), (1, 2), (0, 1), (0, 2), (1, 3), (0, 3)]
    for line, k in coming:
        block = block_of(k, c, (oh, hs)[line])
        if line:
            arrived(r.at[block], xsnd.at[k - 1], xrcv.at[k - 1])
        else:
            for half in range(2):
                arrived(r.at[block, pl.ds(128 * half, 128)], fs.at[k, half], fr.at[k, half])
        slot = k if line else 4 + k
        send(r.at[block], r.at[block], cs.at[slot], cr.at[slot], partner)
    total = term(own)
    for line, k in coming:
        total = total + term(block_of(k, c, (oh, hs)[line]))
    for line, k in [(1, 0)] + coming:
        slot = k if line else 4 + k
        block = block_of(k, 1 - c, (oh, hs)[line])
        arrived(r.at[block], cs.at[slot], cr.at[slot])
        total = total + term(block)
    out[...] = (total * jax.nn.sigmoid(total)).astype(BF16)
    for copy in sent:
        copy.wait_send()


def on_device(nz, source_keys, source_values, queries, fast_weights, step_size, edit_mask, out_proj):
    rows, width = source_keys.shape
    dma = pltpu.SemaphoreType.DMA
    hbm = pl.BlockSpec(memory_space=pl.ANY)
    smem = pl.BlockSpec(memory_space=pltpu.SMEM)

    def body(*refs):
        kernel(nz, *refs)

    return pl.pallas_call(
        body,
        out_shape=pltpu.VMEM((rows, width), BF16),
        in_specs=[hbm, hbm, hbm, hbm, smem, pl.BlockSpec(memory_space=pltpu.HBM), hbm],
        out_specs=pl.BlockSpec(memory_space=pltpu.VMEM),
        scratch_shapes=[
            pltpu.VMEM((2, 256, 128), BF16),
            pltpu.VMEM((2, 256, 128), BF16),
            pltpu.VMEM((2, 256, 128), BF16),
            pltpu.VMEM((256, 128), BF16),
            pltpu.VMEM((2, 256, 128), BF16),
            pltpu.VMEM((2, 3, 128, 256), F32),
            pltpu.VMEM((2048, 256), BF16),
            pltpu.SMEM((1,), jnp.int32),
            pltpu.VMEM((2, 3, 128, 256), F32),
            pltpu.VMEM((2, 4, 2, 3, 16, 256), BF16),
            pltpu.VMEM((2, 3, 2, 3, 16, 256), BF16),
            pltpu.VMEM((2, 2, 3, 16, 256), BF16),
            pltpu.VMEM((2, 3, 16, 256), BF16),
            pltpu.VMEM((3, 2, 3, 16, 256), BF16),
            pltpu.VMEM((2, 4, 2, 3, 16, 256), BF16),
            pltpu.VMEM((3, 128, 512), BF16),
            pltpu.VMEM((256, 128), BF16),
            pltpu.VMEM((16, 256, 128), BF16),
            dma((8,)), dma((3,)), dma((3,)), dma((2, 5)), dma((2, 5)), dma((3,)), dma((3,)),
            dma((9,)), dma((9,)), dma((4, 2)), dma((4, 2)), dma((3,)), dma((3,)), dma((8,)), dma((8,)),
            pltpu.SemaphoreType.REGULAR, pltpu.SemaphoreType.REGULAR, pltpu.SemaphoreType.REGULAR,
        ],
        compiler_params=pltpu.CompilerParams(collective_id=0, has_side_effects=True),
        name="lact_step",
    )(source_keys, source_values, queries, fast_weights, step_size, edit_mask, out_proj)


def solution(mesh):
    nz = mesh.shape["tok"] // NY
    in_specs = (
        P("tok", "head"),
        P("tok", "head"),
        P("tok", "head"),
        P(None, "head", None, None),
        P("head"),
        P("tok"),
        P(None, "head"),
    )

    def device_step(*args):
        return on_device(nz, *args)

    return jax.shard_map(
        device_step, mesh=mesh, in_specs=in_specs, out_specs=P("tok", "head"), check_vma=False
    )
```

```python
import jax
import jax.numpy as jnp
from jax import lax
from jax.experimental import pallas as pl
from jax.experimental.pallas import tpu as pltpu
from jax.sharding import PartitionSpec as P

ITERS = 5
NY = 4
NX = 4
WIN = 4

coef_a = 3.4445
coef_b = -4.775
coef_c = 2.0315

MESH = pl.DeviceIdType.MESH
F32 = jnp.float32
BF16 = jnp.bfloat16


def dot(a, b):
    return jnp.dot(a, b, preferred_element_type=F32)


def dot_nt(a, b):
    return lax.dot_general(a, b, (((1,), (1,)), ((), ())), preferred_element_type=F32)


def dot_tn(a, b):
    return lax.dot_general(a, b, (((0,), (0,)), ((), ())), preferred_element_type=F32)


def split(a):
    high = a.astype(BF16)
    return high, (a - high.astype(F32)).astype(BF16)


def three(left, right):
    return dot(
        jnp.concatenate([left[0], left[1], left[0]], axis=1),
        jnp.concatenate([right[0], right[0], right[1]], axis=0),
    )


def orthogonalize(grads):
    rows = grads[0].shape[0]
    on_diagonal = lax.broadcasted_iota(jnp.int32, (rows, rows), 0) == lax.broadcasted_iota(
        jnp.int32, (rows, rows), 1
    )
    eye = jnp.where(on_diagonal, coef_a, 0.0)
    raw = [dot_nt(g, g) for g in grads]
    scales = [
        lax.rsqrt(jnp.sum(jnp.where(on_diagonal, gram, 0.0), keepdims=True) + 1e-06) for gram in raw
    ]
    grams = [gram * (scale * scale) for gram, scale in zip(raw, scales)]
    factors = [None for _ in grads]
    for sweep in range(ITERS):
        halves = [split(gram) for gram in grams]
        squares = [three(half, half) for half in halves]
        polys = [
            split(eye + coef_b * gram + coef_c * square) for gram, square in zip(grams, squares)
        ]
        if sweep == ITERS - 1:
            return [
                three(poly, split(moved)) * scale for poly, moved, scale in zip(polys, parts, scales)
            ]
        if sweep == 0:
            products = [three(poly, half) for poly, half in zip(polys, halves)]
            factors = polys
        else:
            both = [
                three(
                    poly,
                    (
                        jnp.concatenate([half[0], factor[0]], axis=1),
                        jnp.concatenate([half[1], factor[1]], axis=1),
                    ),
                )
                for poly, half, factor in zip(polys, halves, factors)
            ]
            products = [pair[:, :rows] for pair in both]
            factors = [split(pair[:, rows:]) for pair in both]
        grams = [three(split(product), poly) for product, poly in zip(products, polys)]
        if sweep == ITERS - 2:
            parts = [
                dot(jnp.concatenate(factor, axis=1), jnp.concatenate([g, g], axis=0))
                for factor, g in zip(factors, grads)
            ]


def kernel(
    nz,
    keys, values, queries, weights, step, mask, proj,
    out,
    kbuf, vraw, vbuf, vother, qbuf, w, pj,
    flag, acc, gb, rz1, rz2, sb, r4, gfull, new, rf, r,
    lsem, p1s, p1r, p2s, p2r, p3s, p3r, p4s, p4r, fs, fr, xsnd, xrcv, cs, cr, e2, e4, e8,
):
    t = lax.axis_index("tok")
    hd = lax.axis_index("head")
    y = t // nz
    z = t - y * nz
    x = hd // 2
    c = hd - 2 * x
    hs = y // 2
    ch = y - 2 * hs
    oh = 1 - hs
    pair = y + 1 - 2 * ch
    outer = NY - 1 - y
    i = lax.rem(z, WIN)

    def dev(yy, zz, xx, cc):
        return (yy * nz + zz, xx * 2 + cc)

    def zp(d):
        return lax.rem(z + d + nz, nz)

    def xp(d):
        return lax.rem(x + d + NX, NX)

    partner = dev(y, z, x, 1 - c)

    def send(src, dst, ss, rs, where):
        copy = pltpu.make_async_remote_copy(
            src_ref=src, dst_ref=dst, send_sem=ss, recv_sem=rs, device_id=where, device_id_type=MESH
        )
        copy.start()
        sent.append(copy)

    def arrived(dst, ss, rs):
        pltpu.make_async_remote_copy(
            src_ref=dst, dst_ref=dst, send_sem=ss, recv_sem=rs, device_id=partner, device_id_type=MESH
        ).wait_recv()

    sent = []

    def local(src, dst, k):
        copy = pltpu.make_async_copy(src, dst, lsem.at[k])
        copy.start()
        return copy

    def cols(a):
        return pl.ds(pl.multiple_of(a * 128, 128), 128)

    barrier = pltpu.get_barrier_semaphore()
    to_outer = dev(outer, z, x, c)
    to_pair = dev(pair, z, x, c)
    beside = [dev(y, zp(d), x, c) for d in (1, -1)] + [dev(y, z, xp(d), c) for d in (1, -1)]
    near = beside + [to_outer, to_pair, partner]
    for peer in near:
        pl.semaphore_signal(barrier, inc=1, device_id=peer, device_id_type=MESH)

    mask_in = local(mask, flag, 7)
    v_out = local(values.at[:, cols(oh)], vraw.at[1], 0)
    v_in = local(values.at[:, cols(hs)], vraw.at[0], 1)
    k_in = local(keys.at[:, cols(hs)], kbuf.at[0], 2)
    w_in = []
    for side in range(2):
        at = pl.ds(256 * side, 256)
        w_in.append(local(weights.at[:, hs, :, at], w.at[side], 3 + side))
    q_in = local(queries.at[:, cols(hs)], qbuf.at[0], 5)
    pj_in = local(proj, pj, 6)
    mask_in.wait()
    keep = flag[0].astype(F32)
    v_out.wait()
    vother[...] = (vraw[1].astype(F32) * keep).astype(BF16)
    v_in.wait()
    vbuf[0] = (vraw[0].astype(F32) * keep).astype(BF16)

    pl.semaphore_wait(barrier, len(near))
    send(keys.at[:, cols(oh)], kbuf.at[1], p1s.at[0], p1r.at[0], to_outer)
    send(vother, vbuf.at[1], p1s.at[1], p1r.at[1], to_outer)
    def tell(sem, peers):
        for peer in peers:
            pl.semaphore_signal(sem, inc=1, device_id=peer, device_id_type=MESH)

    tell(e2, beside)

    k_in.wait()
    for copy in w_in:
        copy.wait()
    ahead, behind, across = (lax.rem(i + d, WIN) for d in (1, 3, 2))
    halves = (ch, 1 - ch)

    def gradients(block, side):
        low = [w[side, m].astype(BF16) for m in range(3)]
        k = kbuf[block]
        vm = vbuf[block]
        g = dot(k, low[0])
        u = dot(k, low[2])
        b = dot(vm, low[1])
        sig = jax.nn.sigmoid(g)
        silu = g * sig
        hid = (silu * u).astype(BF16)
        dg = (b * u * (sig * (1.0 + g * (1.0 - sig)))).astype(BF16)
        du = (b * silu).astype(BF16)
        return dot_tn(k, dg), dot_tn(vm, hid), dot_tn(k, du)

    for dy in (1, 0):
        terms = gradients(0, halves[dy])
        for m in range(3):
            acc[dy, m] = terms[m]
        if dy:
            pl.semaphore_wait(e2, len(beside))
            tell(e4, [dev(y, zp(d), x, c) for d in (2, -2)] + [to_pair, to_outer])
    pl.semaphore_wait(e4, 4)
    tell(e8, [dev(y, zp(d), x, c) for d in (4, -4)])
    for k in range(2):
        arrived((kbuf, vbuf)[k].at[1], p1s.at[k], p1r.at[k])
    for dy, yy in ((1, pair), (0, y)):
        terms = gradients(1, halves[dy])
        for m in range(3):
            total = acc[dy, m] + terms[m]
            if dy == 0:
                acc[dy, m] = total
            for j in range(WIN):
                for half in range(2):
                    at = 32 * j + 16 * half
                    gb[dy, j, half, m] = total[at : at + 16, :].astype(BF16)
        ss, rs = p2s.at[dy], p2r.at[dy]
        send(gb.at[dy, across, 0], rz2.at[dy, 0], ss.at[3], rs.at[3], dev(yy, zp(2), x, c))
        send(gb.at[dy, across, 1], rz2.at[dy, 1], ss.at[4], rs.at[4], dev(yy, zp(-2), x, c))
        send(gb.at[dy, ahead], rz1.at[dy, 1], ss.at[1], rs.at[1], dev(yy, zp(1), x, c))
        send(gb.at[dy, behind], rz1.at[dy, 2], ss.at[2], rs.at[2], dev(yy, zp(-1), x, c))
        if dy:
            send(gb.at[dy, i], rz1.at[dy, 0], ss.at[0], rs.at[0], dev(yy, z, x, c))
    send(queries.at[:, cols(oh)], qbuf.at[1], p1s.at[2], p1r.at[2], to_outer)
    pl.semaphore_wait(e8, 2)
    for dy in range(2):
        ss, rs = p2s.at[dy], p2r.at[dy]
        for k in range(3):
            if dy or k:
                arrived(rz1.at[dy, k], ss.at[k], rs.at[k])
        for k in range(2):
            arrived(rz2.at[dy, k], ss.at[3 + k], rs.at[3 + k])
    sums = {}
    for half in range(2):
        for m in range(3):
            rows = pl.ds(pl.multiple_of(i * 32 + 16 * half, 16), 16)
            total = acc[0, m, rows, :]
            for dy in range(2):
                for k in range(3):
                    if dy or k:
                        total = total + rz1[dy, k, half, m].astype(F32)
                total = total + rz2[dy, half, m].astype(F32)
            sums[half, m] = total
            sb[half, m] = total.astype(BF16)
    send(sb, r4.at[2], p3s.at[2], p3r.at[2], dev(y, zp(8), x, c))
    sent.pop().wait_send()
    send(sb, r4.at[0], p3s.at[0], p3r.at[0], dev(y, zp(4), x, c))
    send(sb, r4.at[1], p3s.at[1], p3r.at[1], dev(y, zp(-4), x, c))

    def norms(a):
        return jnp.sqrt(jnp.sum(a * a, axis=0, keepdims=True) + 1e-06)

    old = [[norms(w[side, m]) for side in range(2)] for m in range(3)]
    for k in range(3):
        arrived(r4.at[k], p3s.at[k], p3r.at[k])
    for half in range(2):
        for m in range(3):
            total = sums[half, m]
            for k in range(3):
                total = total + r4[k, half, m].astype(F32)
            gfull[ch, i, half, m] = total.astype(BF16)
    mine, first, second = gfull.at[ch, i], gfull.at[ch, i, 0], gfull.at[ch, i, 1]
    for base, yy in ((4, pair), (0, y)):
        send(first, first, p4s.at[base + 2], p4r.at[base + 2], dev(yy, zp(2), x, c))
        send(second, second, p4s.at[base + 3], p4r.at[base + 3], dev(yy, zp(-2), x, c))
        send(mine, mine, p4s.at[base], p4r.at[base], dev(yy, zp(1), x, c))
        send(mine, mine, p4s.at[base + 1], p4r.at[base + 1], dev(yy, zp(-1), x, c))
    send(mine, mine, p4s.at[8], p4r.at[8], dev(pair, z, x, c))
    arrived(gfull.at[1 - ch, i], p4s.at[8], p4r.at[8])
    for base, side in ((0, ch), (4, 1 - ch)):
        arrived(gfull.at[side, behind], p4s.at[base], p4r.at[base])
        arrived(gfull.at[side, ahead], p4s.at[base + 1], p4r.at[base + 1])
        arrived(gfull.at[side, across, 0], p4s.at[base + 2], p4r.at[base + 2])
        arrived(gfull.at[side, across, 1], p4s.at[base + 3], p4r.at[base + 3])
    grads = []
    for m in range(3):
        columns = [
            jnp.concatenate(
                [gfull[side, j, half, m] for j in range(WIN) for half in range(2)], axis=0
            )
            for side in range(2)
        ]
        grads.append(jnp.concatenate(columns, axis=1))
    directions = orthogonalize(grads)

    rate = step[hs]
    for m in range(3):
        for side in range(2):
            at = slice(256 * side, 256 * side + 256)
            proposed = w[side, m] + rate * directions[m][:, at]
            new[m, :, at] = (proposed * (old[m][side] / norms(proposed))).astype(BF16)

    def read_of(q):
        rg = dot(q, new[0])
        ru = dot(q, new[2])
        rh = (rg * jax.nn.sigmoid(rg) * ru).astype(BF16)
        return dot_nt(rh, new[1]).astype(BF16)

    around = (0, 1, -1, 2)
    own = 2 * hd + hs
    arrived(qbuf.at[1], p1s.at[2], p1r.at[2])
    for half in range(2):
        part = pl.ds(128 * half, 128)
        rf[part, :] = read_of(qbuf[1, part, :])
        for k in (3, 1, 2):
            where = dev(outer, z, xp(around[k]), c)
            send(rf.at[part], r.at[own, part], fs.at[k, half], fr.at[k, half], where)
    for half in range(2):
        part = pl.ds(128 * half, 128)
        send(rf.at[part], r.at[own, part], fs.at[0, half], fr.at[0, half], to_outer)
    q_in.wait()
    r[own] = read_of(qbuf[0])
    for k in (3, 1, 2):
        send(r.at[own], r.at[own], xsnd.at[k - 1], xrcv.at[k - 1], dev(y, z, xp(around[k]), c))
    send(r.at[own], r.at[own], cs.at[0], cr.at[0], partner)
    pj_in.wait()

    def term(block):
        return dot(r[block], pj[pl.ds(pl.multiple_of(block * 128, 128), 128), :])

    def block_of(k, cc, head):
        return 2 * (2 * xp(-around[k]) + cc) + head

    coming = [(0, 0), (1, 1), (1, 2), (0, 1), (0, 2), (1, 3), (0, 3)]
    for line, k in coming:
        block = block_of(k, c, (oh, hs)[line])
        if line:
            arrived(r.at[block], xsnd.at[k - 1], xrcv.at[k - 1])
        else:
            for half in range(2):
                arrived(r.at[block, pl.ds(128 * half, 128)], fs.at[k, half], fr.at[k, half])
        slot = k if line else 4 + k
        send(r.at[block], r.at[block], cs.at[slot], cr.at[slot], partner)
    total = term(own)
    for line, k in coming:
        total = total + term(block_of(k, c, (oh, hs)[line]))
    for line, k in [(1, 0)] + coming:
        slot = k if line else 4 + k
        block = block_of(k, 1 - c, (oh, hs)[line])
        arrived(r.at[block], cs.at[slot], cr.at[slot])
        total = total + term(block)
    out[...] = (total * jax.nn.sigmoid(total)).astype(BF16)
    for copy in sent:
        copy.wait_send()


def on_device(nz, source_keys, source_values, queries, fast_weights, step_size, edit_mask, out_proj):
    rows, width = source_keys.shape
    dma = pltpu.SemaphoreType.DMA
    hbm = pl.BlockSpec(memory_space=pl.ANY)
    smem = pl.BlockSpec(memory_space=pltpu.SMEM)

    def body(*refs):
        kernel(nz, *refs)

    return pl.pallas_call(
        body,
        out_shape=pltpu.VMEM((rows, width), BF16),
        in_specs=[hbm, hbm, hbm, hbm, smem, pl.BlockSpec(memory_space=pltpu.HBM), hbm],
        out_specs=pl.BlockSpec(memory_space=pltpu.VMEM),
        scratch_shapes=[
            pltpu.VMEM((2, 256, 128), BF16),
            pltpu.VMEM((2, 256, 128), BF16),
            pltpu.VMEM((2, 256, 128), BF16),
            pltpu.VMEM((256, 128), BF16),
            pltpu.VMEM((2, 256, 128), BF16),
            pltpu.VMEM((2, 3, 128, 256), F32),
            pltpu.VMEM((2048, 256), BF16),
            pltpu.SMEM((1,), jnp.int32),
            pltpu.VMEM((2, 3, 128, 256), F32),
            pltpu.VMEM((2, 4, 2, 3, 16, 256), BF16),
            pltpu.VMEM((2, 3, 2, 3, 16, 256), BF16),
            pltpu.VMEM((2, 2, 3, 16, 256), BF16),
            pltpu.VMEM((2, 3, 16, 256), BF16),
            pltpu.VMEM((3, 2, 3, 16, 256), BF16),
            pltpu.VMEM((2, 4, 2, 3, 16, 256), BF16),
            pltpu.VMEM((3, 128, 512), BF16),
            pltpu.VMEM((256, 128), BF16),
            pltpu.VMEM((16, 256, 128), BF16),
            dma((8,)), dma((3,)), dma((3,)), dma((2, 5)), dma((2, 5)), dma((3,)), dma((3,)),
            dma((9,)), dma((9,)), dma((4, 2)), dma((4, 2)), dma((3,)), dma((3,)), dma((8,)), dma((8,)),
            pltpu.SemaphoreType.REGULAR, pltpu.SemaphoreType.REGULAR, pltpu.SemaphoreType.REGULAR,
        ],
        compiler_params=pltpu.CompilerParams(collective_id=0, has_side_effects=True),
        name="lact_step",
    )(source_keys, source_values, queries, fast_weights, step_size, edit_mask, out_proj)


def solution(mesh):
    nz = mesh.shape["tok"] // NY
    in_specs = (
        P("tok", "head"),
        P("tok", "head"),
        P("tok", "head"),
        P(None, "head", None, None),
        P("head"),
        P("tok"),
        P(None, "head"),
    )

    def device_step(*args):
        return on_device(nz, *args)

    return jax.shard_map(
        device_step, mesh=mesh, in_specs=in_specs, out_specs=P("tok", "head"), check_vma=False
    )
```
